512 devices in a mesh: wide: 32 (over y, z_lo, core), narrow: 16 (over z_hi, x).
Axes of the slice: x: 4, y: 8, z: 8 (z_hi: 4, z_lo: 2; z = z_hi * 2 + z_lo), core: 2. Of those that a mesh axis runs over, the one named last changes fastest.
Arguments:
- beams: bfloat16 [128, 256, 256], P('narrow'), may hold values from -0.375 to 0.375
- basis: bfloat16 [32768, 128], P('wide'), may hold values from -0.375 to 0.375
- foreground: float32 [128, 128, 256], P('narrow', 'wide'), may hold values from 0.3 to 3
- signal: float32 [128, 128, 256], P('narrow', 'wide'), may hold values from 0.3 to 3
- band_start: int32 [128], P('narrow'), may hold values from 0 to 96, as said below
- band_width: int32 [128], P('narrow'), may hold values from 32 to 128
Outputs:
- projected_rows: float32 [32768, 128], P(('wide', 'narrow'))
- kl_matrix: float32 [128, 128], replicated
The draws below stay inside these ranges and needn't reach their ends.
Inputs may be any that keep to these rules, and one draw needn't show every extreme that they name: band_start + band_width <= 128 in every block row.
All inputs are finite; a program needn't handle non-finite values.
Results may differ from the reference program's by a relative error of at most 0.0041.
Values may be sent and summed in bfloat16 or wider, within the bound.
A program may use at most 64 MiB of HBM per device.

```python
import math
import jax
import jax.numpy as jnp
from jax import lax

NFREQ = 128
NBEAM = 256
NL = 256
KL = 128
NMODES = 32768


def band_pair(key):
    base = jax.random.fold_in(key, 11)
    width = jax.random.randint(jax.random.fold_in(base, 1), (NFREQ,), NFREQ // 4, NFREQ + 1)
    room = NFREQ - width + 1
    start = jax.random.randint(jax.random.fold_in(base, 2), (NFREQ,), 0, 2 ** 30) % room
    chosen = jax.random.randint(jax.random.fold_in(base, 3), (), 0, NFREQ)
    second = (chosen + 1 + jax.random.randint(jax.random.fold_in(base, 4), (), 0, NFREQ - 1)) % NFREQ
    places = jnp.arange(NFREQ, dtype=jnp.int32)
    width = jnp.where(places == chosen, NFREQ, width)
    start = jnp.where(places == chosen, 0, start)
    width = jnp.where(places == second, NFREQ // 4, width)
    start = jnp.where(places == second, NFREQ - NFREQ // 4, start)
    return (start.astype(jnp.int32), width.astype(jnp.int32))


def draw_band_start(key, part):
    return band_pair(key)[0]


def draw_band_width(key, part):
    return band_pair(key)[1]


def levels(own_key, extent, split, smallest, high):
    def one(axis_at, blocks):
        heights = jax.random.uniform(jax.random.fold_in(jax.random.fold_in(own_key, 6), axis_at), (blocks,), jnp.float32, smallest / len(split), high / len(split))
        return jnp.repeat(jnp.exp(heights), extent[axis_at] // blocks).reshape((-1,) + (1,) * (len(extent) - axis_at - 1))

    level = one(*split[0])
    for cut in split[1:]:
        level = level * one(*cut)
    return level


def centred(rng, extent, deviation, most, shards=(), kind=jnp.bfloat16):
    entries = jax.random.normal(rng, extent, jnp.float32) * deviation
    if len(shards) > 0:
        entries = levels(rng, extent, shards, -0.22, 0.18) * entries
    return jnp.clip(entries, min=-most, max=most).astype(kind)


def setup_inputs(seed: int = 0) -> dict:
    key_of = jax.random.split(jax.random.key(seed), 7)
    return {
        "beams": centred(key_of[0], (NFREQ, NBEAM, NL), NL ** -0.5, 0.375, ((0, 16),)),
        "basis": centred(key_of[1], (NMODES, KL), NBEAM ** -0.5, 0.375, ((0, 32),)),
        "foreground": jnp.clip(jnp.exp(math.log(3.0) - 2.3025851 * jax.random.uniform(key_of[2], (NFREQ, NFREQ, NL), jnp.float32) ** levels(key_of[2], (NFREQ, NFREQ, NL), ((0, 16), (1, 32)), -0.2, 0.2)), 0.3, 3.0),
        "signal": jnp.clip(jnp.exp(math.log(3.0) - 2.3025851 * jax.random.uniform(key_of[3], (NFREQ, NFREQ, NL), jnp.float32) ** levels(key_of[3], (NFREQ, NFREQ, NL), ((0, 16), (1, 32)), -0.2, 0.2)), 0.3, 3.0),
        "band_start": draw_band_start(jax.random.fold_in(key_of[6], 71), 0),
        "band_width": draw_band_width(jax.random.fold_in(key_of[6], 71), 0),
    }


def reference(beams, basis, foreground, signal, band_start, band_width):
    freq = jnp.arange(NFREQ, dtype=jnp.int32)
    inband = ((freq[None, :] >= band_start[:, None]) & (freq[None, :] < (band_start + band_width)[:, None])).astype(jnp.float32)
    basis_blocks = basis.reshape(NFREQ, NBEAM, KL)
    beams_wide = beams.astype(jnp.float32)

    def one_row(total, items):
        beam_row, fore_row, sig_row, band_row, basis_row = items
        spectrum = fore_row + band_row[:, None] * sig_row
        scaled = (beam_row.astype(jnp.float32)[None, :, :] * spectrum[:, None, :]).astype(jnp.bfloat16)
        scaled = lax.optimization_barrier(scaled).astype(jnp.float32)
        block = jnp.einsum("gbl,gcl->gbc", scaled, beams_wide).astype(jnp.bfloat16)
        block = lax.optimization_barrier(block).astype(jnp.float32)
        contrib = jnp.einsum("gbc,bk->gck", block, basis_row.astype(jnp.float32))
        return total + contrib, None

    start = jnp.zeros((NFREQ, NBEAM, KL), jnp.float32)
    total, _ = lax.scan(one_row, start, (beams, foreground, signal, inband, basis_blocks))
    projected_rows = total.reshape(NFREQ * NBEAM, KL)
    kl_matrix = jnp.dot(projected_rows.T, basis.astype(jnp.float32), precision=lax.Precision.HIGH, preferred_element_type=jnp.float32) / NFREQ
    return projected_rows, kl_matrix
```

```python
import jax
import jax.numpy as jnp
from jax import lax
from jax.experimental import pallas as pl
from jax.experimental.pallas import tpu as pltpu
from jax.sharding import PartitionSpec as P

MESH = pl.DeviceIdType.MESH
F32 = jnp.float32
BF16 = jnp.bfloat16
NT = (((1,), (1,)), ((), ()))


def nt(a, b):
    return lax.dot_general(a, b, NT, preferred_element_type=F32)


def split(value):
    high = value.astype(BF16)
    return high, (value - high.astype(F32)).astype(BF16)


def put(src, dst, send, recv, device):
    return pltpu.make_async_remote_copy(
        src_ref=src, dst_ref=dst, send_sem=send, recv_sem=recv, device_id=device, device_id_type=MESH
    )


def drain(ref, sem):
    pltpu.make_async_copy(ref, ref, sem).wait()


def kernel(
    beams_hbm, basis_hbm, fore_hbm, sig_hbm, start_ref, width_ref, proj_ref, kl_ref,
    beams_v, basis_v, fore_v, sig_v, basis_t, basis_in, beam_in, spec, part, got, mine, rows, term, got5, own6, got6, kl_v,
    local, send, recv,
):
    w = lax.axis_index("wide")
    n = lax.axis_index("narrow")
    y, q = lax.div(w, 4), lax.rem(w, 4)
    z, x = lax.div(n, 4), lax.rem(n, 4)
    chip, core = lax.div(w, 2), lax.rem(w, 2)
    g = x * 4 + q
    h = y * 4 + z
    diagonal = chip == n

    load_basis = pltpu.make_async_copy(basis_hbm, basis_v, local.at[0])
    load_fore = pltpu.make_async_copy(fore_hbm, fore_v, local.at[1])
    load_sig = pltpu.make_async_copy(sig_hbm, sig_v, local.at[2])
    load_beams = pltpu.make_async_copy(beams_hbm, beams_v, local.at[3])
    load_basis.start()
    load_fore.start()
    load_sig.start()
    load_beams.start()

    def in_narrow(i):
        other = lax.rem(n + i, 16)
        return other, (w, other)

    def in_group(i):
        other = lax.rem(g + i, 16)
        return other, (y * 4 + lax.rem(other, 4), z * 4 + lax.div(other, 4))

    def in_rest(i):
        other = lax.rem(h + i, 32)
        return other, (lax.div(other, 4) * 4 + q, lax.rem(other, 4) * 4 + x)

    barrier = pltpu.get_barrier_semaphore()

    def greet(device):
        pl.semaphore_signal(barrier, inc=1, device_id=device, device_id_type=MESH)

    @pl.loop(1, 16)
    def _(i):
        greet(in_narrow(i)[1])
        greet(in_group(i)[1])

    @pl.loop(1, 32)
    def _(i):
        greet(in_rest(i)[1])

    greet((2 * n + 1 - core, chip))

    @pl.when(jnp.logical_not(diagonal))
    def _():
        greet((2 * n + core, chip))

    load_fore.wait()
    load_sig.wait()
    column = 4 * w + lax.broadcasted_iota(jnp.int32, (4, 256), 0)
    for f in range(8):
        low = start_ref[f]
        inband = ((column >= low) & (column < low + width_ref[f])).astype(F32)
        spec[q, pl.ds(4 * f, 4), :] = fore_v[f] + inband * sig_v[f]
    load_basis.wait()
    for f in range(4):
        basis_t[f] = basis_v[pl.ds(256 * f, 256), :].astype(F32).T.astype(BF16)
    load_beams.wait()

    pl.semaphore_wait(barrier, 63 - diagonal.astype(jnp.int32))

    for i in range(1, 4):
        put(spec.at[q], spec.at[q], send.at[0], recv.at[0], (y * 4 + lax.rem(q + i, 4), n)).start()
    far_half = 2 * lax.rem(n, 2)
    beam_src = beams_v.at[4 * core + lax.div(chip, 4), pl.ds(64 * lax.rem(chip, 4), 64), :]

    def basis_src(to_core):
        return basis_t.at[:, pl.ds(32 * (far_half + to_core), 32), :]

    put(basis_src(1 - core), basis_in.at[core], send.at[1], recv.at[1], (2 * n + 1 - core, chip)).start()

    @pl.when(diagonal)
    def _():
        pltpu.make_async_copy(basis_src(core), basis_in.at[core], recv.at[1]).start()
        pltpu.make_async_copy(beam_src, beam_in, recv.at[2]).start()

    @pl.when(jnp.logical_not(diagonal))
    def _():
        put(basis_src(core), basis_in.at[core], send.at[2], recv.at[1], (2 * n + core, chip)).start()
        put(beam_src, beam_in, send.at[3], recv.at[2], (2 * n + core, chip)).start()

    drain(spec.at[pl.ds(0, 3)], recv.at[0])
    drain(basis_in, recv.at[1])

    made = [
        jnp.dot(basis_in[f // 4, f % 4], beams_v[f], preferred_element_type=F32) for f in range(8)
    ]
    for j in range(4):
        for pair in range(2):
            halves = []
            for r in range(2 * pair, 2 * pair + 2):
                total = spec[r, pl.ds(j, 1), :] * made[0]
                for f in range(1, 8):
                    total = total + spec[r, pl.ds(4 * f + j, 1), :] * made[f]
                halves.append(total)
            for xx in range(4):
                piece = jnp.concatenate([half[8 * xx : 8 * xx + 8] for half in halves], axis=0)
                part[4 * j + xx, pl.ds(16 * pair, 16), :] = piece.astype(BF16)

    @pl.loop(1, 16)
    def _(i):
        other, device = in_narrow(i)
        put(part.at[other], got.at[n], send.at[4], recv.at[3], device).start()

    got[n] = part[n]
    drain(got.at[pl.ds(0, 15)], recv.at[3])
    total = got[0].astype(F32)
    for i in range(1, 16):
        total = total + got[i].astype(F32)
    mine[...] = total

    place = pl.multiple_of(32 * q + 8 * x, 8)

    @pl.loop(1, 16)
    def _(i):
        other, device = in_group(i)
        source = mine.at[pl.ds(pl.multiple_of(8 * lax.rem(other, 4), 8), 8), :]
        put(source, rows.at[pl.ds(place, 8), :], send.at[5], recv.at[4], device).start()

    rows[pl.ds(place, 8), :] = mine[pl.ds(pl.multiple_of(8 * q, 8), 8), :]
    drain(beam_in, recv.at[2])
    drain(rows.at[pl.ds(0, 120)], recv.at[4])

    high, low = split(rows[...])
    chunk = beam_in[...]
    turned = nt(high, chunk) + nt(low, chunk)
    local_basis = basis_v[pl.ds(pl.multiple_of(64 * n, 64), 64), :]
    turned_high, turned_low = split(turned)
    term[...] = jnp.dot(turned_high, local_basis, preferred_element_type=F32) + jnp.dot(
        turned_low, local_basis, preferred_element_type=F32
    )

    @pl.loop(1, 16)
    def _(i):
        other, device = in_group(i)
        source = term.at[pl.ds(pl.multiple_of(8 * other, 8), 8), :]
        put(source, got5.at[g], send.at[6], recv.at[5], device).start()

    got5[g] = term[pl.ds(pl.multiple_of(8 * g, 8), 8), :]
    proj_ref[...] = nt(chunk, high) + nt(chunk, low)
    drain(got5.at[pl.ds(0, 15)], recv.at[5])
    total = got5[0]
    for i in range(1, 16):
        total = total + got5[i]
    own6[...] = total

    @pl.loop(1, 32)
    def _(i):
        other, device = in_rest(i)
        put(own6, got6.at[h], send.at[7], recv.at[6], device).start()

    got6[h] = total
    drain(got6.at[pl.ds(0, 31)], recv.at[6])
    total = got6[0]
    for i in range(1, 32):
        total = total + got6[i]
    here = kl_v.at[pl.ds(pl.multiple_of(8 * g, 8), 8), :]
    here[...] = total * (1.0 / 128)

    @pl.loop(1, 16)
    def _(i):
        other, device = in_group(i)
        put(here, here, send.at[8], recv.at[7], device).start()

    drain(kl_v.at[pl.ds(0, 120)], recv.at[7])
    kl_ref[...] = kl_v[...]

    drain(spec.at[pl.ds(0, 3)], send.at[0])
    drain(basis_in.at[0], send.at[1])

    @pl.when(jnp.logical_not(diagonal))
    def _():
        drain(basis_in.at[0], send.at[2])
        drain(beam_in, send.at[3])

    drain(got.at[pl.ds(0, 15)], send.at[4])
    drain(rows.at[pl.ds(0, 120)], send.at[5])
    drain(got5.at[pl.ds(0, 15)], send.at[6])
    drain(got6.at[pl.ds(0, 31)], send.at[7])
    drain(kl_v.at[pl.ds(0, 120)], send.at[8])


def per_device(beams, basis, foreground, signal, band_start, band_width):
    anywhere = pl.BlockSpec(memory_space=pl.ANY)
    scalars = pl.BlockSpec(memory_space=pltpu.SMEM)
    vector = pl.BlockSpec(memory_space=pltpu.VMEM)
    return pl.pallas_call(
        kernel,
        out_shape=(
            jax.ShapeDtypeStruct((64, 128), F32),
            jax.ShapeDtypeStruct((128, 128), F32),
        ),
        in_specs=[anywhere] * 4 + [scalars] * 2,
        out_specs=(vector, vector),
        scratch_shapes=[
            pltpu.VMEM((8, 256, 256), BF16),
            pltpu.VMEM((1024, 128), BF16),
            pltpu.VMEM((8, 4, 256), F32),
            pltpu.VMEM((8, 4, 256), F32),
            pltpu.VMEM((4, 128, 256), BF16),
            pltpu.VMEM((2, 4, 32, 256), BF16),
            pltpu.VMEM((64, 256), BF16),
            pltpu.VMEM((4, 32, 256), F32),
            pltpu.VMEM((16, 32, 256), BF16),
            pltpu.VMEM((16, 32, 256), BF16),
            pltpu.VMEM((32, 256), F32),
            pltpu.VMEM((128, 256), F32),
            pltpu.VMEM((128, 128), F32),
            pltpu.VMEM((16, 8, 128), F32),
            pltpu.VMEM((8, 128), F32),
            pltpu.VMEM((32, 8, 128), F32),
            pltpu.VMEM((128, 128), F32),
            pltpu.SemaphoreType.DMA((4,)),
            pltpu.SemaphoreType.DMA((9,)),
            pltpu.SemaphoreType.DMA((8,)),
        ],
        compiler_params=pltpu.CompilerParams(
            collective_id=0, has_side_effects=True, vmem_limit_bytes=32 << 20
        ),
    )(beams, basis, foreground, signal, band_start, band_width)


def solution(mesh):
    placed = (
        P("narrow", None, None),
        P("wide", None),
        P("narrow", "wide", None),
        P("narrow", "wide", None),
        P("narrow"),
        P("narrow"),
    )
    return jax.shard_map(
        per_device,
        mesh=mesh,
        in_specs=placed,
        out_specs=(P(("wide", "narrow"), None), P()),
        check_vma=False,
    )
```

```python
import jax
import jax.numpy as jnp
from jax import lax
from jax.experimental import pallas as pl
from jax.experimental.pallas import tpu as pltpu
from jax.sharding import PartitionSpec as P

MESH = pl.DeviceIdType.MESH
F32 = jnp.float32
BF16 = jnp.bfloat16
NT = (((1,), (1,)), ((), ()))


def nt(a, b):
    return lax.dot_general(a, b, NT, preferred_element_type=F32)


def split(value):
    high = value.astype(BF16)
    return high, (value - high.astype(F32)).astype(BF16)


def put(src, dst, send, recv, device):
    return pltpu.make_async_remote_copy(
        src_ref=src, dst_ref=dst, send_sem=send, recv_sem=recv, device_id=device, device_id_type=MESH
    )


def drain(ref, sem):
    pltpu.make_async_copy(ref, ref, sem).wait()


def kernel(
    beams_hbm, basis_hbm, fore_hbm, sig_hbm, start_ref, width_ref, proj_ref, kl_ref,
    beam_v, block_v, basis_v, fore_v, sig_v, basis_t, basis_in, made, beam_in, spec, part, got, mine, rows, term,
    got5, got6, got7, kl_v, local, send, recv,
):
    w = lax.axis_index("wide")
    n = lax.axis_index("narrow")
    y, q = lax.div(w, 4), lax.rem(w, 4)
    z, x = lax.div(n, 4), lax.rem(n, 4)
    chip, core = lax.div(w, 2), lax.rem(w, 2)
    g = x * 4 + q

    to_f = lax.rem(z - lax.div(chip, 4) + 4, 4)
    to_y = 4 * core + to_f
    to_q = lax.rem(x - lax.rem(chip, 4) - core + 9, 4)
    turn = lax.rem(y - lax.div(n, 2) + 8, 8)
    to_core, to_z = lax.rem(turn, 2), lax.div(turn, 2)
    to_x = 2 * lax.rem(q, 2) + 1 - lax.div(q, 2)
    basis_target = (4 * to_y + to_q, chip)
    beam_target = (2 * n + to_core, 4 * to_z + to_x)
    high_y = lax.div(y, 4)
    basis_source = (2 * n + high_y, 4 * lax.rem(y + z, 4) + lax.rem(q + high_y + 3 + x, 4))
    beam_source = (4 * lax.rem(y + 2 * z + core, 8) + 2 * (1 - lax.rem(x, 2)) + lax.div(x, 2), chip)

    load_block = pltpu.make_async_copy(
        basis_hbm.at[pl.ds(pl.multiple_of(256 * to_f, 256), 256), :], block_v, local.at[0]
    )
    load_fore = pltpu.make_async_copy(fore_hbm, fore_v, local.at[1])
    load_sig = pltpu.make_async_copy(sig_hbm, sig_v, local.at[2])
    load_beam = pltpu.make_async_copy(beams_hbm.at[y], beam_v, local.at[3])
    load_basis = pltpu.make_async_copy(
        basis_hbm.at[pl.ds(pl.multiple_of(64 * n, 64), 64), :], basis_v, local.at[4]
    )
    load_block.start()
    load_fore.start()
    load_sig.start()
    load_beam.start()
    load_basis.start()

    def in_narrow(i):
        other = lax.rem(n + i, 16)
        return other, (w, other)

    def in_group(i):
        other = lax.rem(g + i, 16)
        return other, (y * 4 + lax.rem(other, 4), z * 4 + lax.div(other, 4))

    def in_y(i):
        return (4 * lax.rem(y + i, 8) + q, n)

    def in_z(i):
        return (w, 4 * lax.rem(z + i, 4) + x)

    barrier = pltpu.get_barrier_semaphore()

    def greet(device):
        pl.semaphore_signal(barrier, inc=1, device_id=device, device_id_type=MESH)

    greet(basis_source)
    greet(beam_source)

    @pl.loop(1, 16)
    def _(i):
        greet(in_group(i)[1])
        greet(in_narrow(i)[1])

    @pl.loop(1, 8)
    def _(i):
        greet(in_y(i))

    load_fore.wait()
    load_sig.wait()
    column = 4 * w + lax.broadcasted_iota(jnp.int32, (4, 256), 0)
    for f in range(8):
        low = start_ref[f]
        inband = ((column >= low) & (column < low + width_ref[f])).astype(F32)
        spec[q, pl.ds(4 * f, 4), :] = fore_v[f] + inband * sig_v[f]
    load_block.wait()
    basis_t[...] = block_v[...].astype(F32).T.astype(BF16)

    pl.semaphore_wait(barrier, 39)

    columns = basis_t.at[pl.ds(pl.multiple_of(32 * to_q, 32), 32), :]
    put(columns, basis_in, send.at[1], recv.at[1], basis_target).start()
    for i in range(1, 4):
        put(spec.at[q], spec.at[q], send.at[0], recv.at[0], (y * 4 + lax.rem(q + i, 4), n)).start()
    chunk_rows = pl.ds(pl.multiple_of(64 * to_x, 64), 64)
    put(beams_hbm.at[4 * to_core + to_z, chunk_rows, :], beam_in, send.at[2], recv.at[2], beam_target).start()

    load_beam.wait()
    drain(basis_in, recv.at[1])
    made[y] = jnp.dot(basis_in[...], beam_v[...], preferred_element_type=F32).astype(BF16)

    for i in range(1, 8):
        put(made.at[y], made.at[y], send.at[3], recv.at[8], in_y(i)).start()
    drain(spec.at[pl.ds(0, 3)], recv.at[0])
    drain(made.at[pl.ds(0, 7)], recv.at[8])

    wide_made = [made[f].astype(F32) for f in range(8)]
    for j in range(4):
        for pair in range(2):
            halves = []
            for r in range(2 * pair, 2 * pair + 2):
                total = spec[r, pl.ds(j, 1), :] * wide_made[0]
                for f in range(1, 8):
                    total = total + spec[r, pl.ds(4 * f + j, 1), :] * wide_made[f]
                halves.append(total)
            for xx in range(4):
                piece = jnp.concatenate([half[8 * xx : 8 * xx + 8] for half in halves], axis=0)
                part[4 * j + xx, pl.ds(16 * pair, 16), :] = piece.astype(BF16)

    @pl.loop(1, 16)
    def _(i):
        other, device = in_narrow(i)
        put(part.at[other], got.at[n], send.at[4], recv.at[3], device).start()

    got[n] = part[n]
    drain(got.at[pl.ds(0, 15)], recv.at[3])
    total = got[0].astype(F32)
    for i in range(1, 16):
        total = total + got[i].astype(F32)
    mine[...] = total

    place = pl.multiple_of(32 * q + 8 * x, 8)

    @pl.loop(1, 16)
    def _(i):
        other, device = in_group(i)
        source = mine.at[pl.ds(pl.multiple_of(8 * lax.rem(other, 4), 8), 8), :]
        put(source, rows.at[pl.ds(place, 8), :], send.at[5], recv.at[4], device).start()

    rows[pl.ds(place, 8), :] = mine[pl.ds(pl.multiple_of(8 * q, 8), 8), :]
    drain(beam_in, recv.at[2])
    drain(rows.at[pl.ds(0, 120)], recv.at[4])

    high, low = split(rows[...])
    chunk = beam_in[...]
    turned = nt(high, chunk) + nt(low, chunk)
    load_basis.wait()
    local_basis = basis_v[...]
    turned_high, turned_low = split(turned)
    term[...] = jnp.dot(turned_high, local_basis, preferred_element_type=F32) + jnp.dot(
        turned_low, local_basis, preferred_element_type=F32
    )

    @pl.loop(1, 16)
    def _(i):
        other, device = in_group(i)
        source = term.at[pl.ds(pl.multiple_of(8 * other, 8), 8), :]
        put(source, got5.at[g], send.at[6], recv.at[5], device).start()

    got5[g] = term[pl.ds(pl.multiple_of(8 * g, 8), 8), :]
    proj_ref[...] = nt(chunk, high) + nt(chunk, low)
    drain(got5.at[pl.ds(0, 15)], recv.at[5])
    total = got5[0]
    for i in range(1, 16):
        total = total + got5[i]
    got6[z] = total
    for i in range(1, 4):
        put(got6.at[z], got6.at[z], send.at[7], recv.at[6], in_z(i)).start()
    drain(got6.at[pl.ds(0, 3)], recv.at[6])
    got7[y] = (got6[0] + got6[1]) + (got6[2] + got6[3])
    for i in range(1, 8):
        put(got7.at[y], got7.at[y], send.at[8], recv.at[7], in_y(i)).start()
    drain(got7.at[pl.ds(0, 7)], recv.at[7])
    total = got7[0]
    for i in range(1, 8):
        total = total + got7[i]
    here = kl_v.at[pl.ds(pl.multiple_of(8 * g, 8), 8), :]
    here[...] = total * (1.0 / 128)

    @pl.loop(1, 16)
    def _(i):
        other, device = in_group(i)
        put(here, here, send.at[9], recv.at[9], device).start()

    drain(kl_v.at[pl.ds(0, 120)], recv.at[9])
    kl_ref[...] = kl_v[...]

    drain(spec.at[pl.ds(0, 3)], send.at[0])
    drain(basis_in, send.at[1])
    drain(beam_in, send.at[2])
    drain(made.at[pl.ds(0, 7)], send.at[3])
    drain(got.at[pl.ds(0, 15)], send.at[4])
    drain(rows.at[pl.ds(0, 120)], send.at[5])
    drain(got5.at[pl.ds(0, 15)], send.at[6])
    drain(got6.at[pl.ds(0, 3)], send.at[7])
    drain(got7.at[pl.ds(0, 7)], send.at[8])
    drain(kl_v.at[pl.ds(0, 120)], send.at[9])


def per_device(beams, basis, foreground, signal, band_start, band_width):
    anywhere = pl.BlockSpec(memory_space=pl.ANY)
    scalars = pl.BlockSpec(memory_space=pltpu.SMEM)
    vector = pl.BlockSpec(memory_space=pltpu.VMEM)
    return pl.pallas_call(
        kernel,
        out_shape=(
            jax.ShapeDtypeStruct((64, 128), F32),
            jax.ShapeDtypeStruct((128, 128), F32),
        ),
        in_specs=[anywhere] * 4 + [scalars] * 2,
        out_specs=(vector, vector),
        scratch_shapes=[
            pltpu.VMEM((256, 256), BF16),
            pltpu.VMEM((256, 128), BF16),
            pltpu.VMEM((64, 128), BF16),
            pltpu.VMEM((8, 4, 256), F32),
            pltpu.VMEM((8, 4, 256), F32),
            pltpu.VMEM((128, 256), BF16),
            pltpu.VMEM((32, 256), BF16),
            pltpu.VMEM((8, 32, 256), BF16),
            pltpu.VMEM((64, 256), BF16),
            pltpu.VMEM((4, 32, 256), F32),
            pltpu.VMEM((16, 32, 256), BF16),
            pltpu.VMEM((16, 32, 256), BF16),
            pltpu.VMEM((32, 256), F32),
            pltpu.VMEM((128, 256), F32),
            pltpu.VMEM((128, 128), F32),
            pltpu.VMEM((16, 8, 128), F32),
            pltpu.VMEM((4, 8, 128), F32),
            pltpu.VMEM((8, 8, 128), F32),
            pltpu.VMEM((128, 128), F32),
            pltpu.SemaphoreType.DMA((5,)),
            pltpu.SemaphoreType.DMA((10,)),
            pltpu.SemaphoreType.DMA((10,)),
        ],
        compiler_params=pltpu.CompilerParams(
            collective_id=0, has_side_effects=True, vmem_limit_bytes=60 << 20
        ),
    )(beams, basis, foreground, signal, band_start, band_width)


def solution(mesh):
    placed = (
        P("narrow", None, None),
        P("wide", None),
        P("narrow", "wide", None),
        P("narrow", "wide", None),
        P("narrow"),
        P("narrow"),
    )
    return jax.shard_map(
        per_device,
        mesh=mesh,
        in_specs=placed,
        out_specs=(P(("wide", "narrow"), None), P()),
        check_vma=False,
    )
```

```python
import jax
import jax.numpy as jnp
from jax import lax
from jax.experimental import pallas as pl
from jax.experimental.pallas import tpu as pltpu
from jax.sharding import PartitionSpec as P

MESH = pl.DeviceIdType.MESH
F32 = jnp.float32
BF16 = jnp.bfloat16
NT = (((1,), (1,)), ((), ()))


def nt(a, b):
    return lax.dot_general(a, b, NT, preferred_element_type=F32)


def split(value):
    high = value.astype(BF16)
    return high, (value - high.astype(F32)).astype(BF16)


def put(src, dst, send, recv, device):
    return pltpu.make_async_remote_copy(
        src_ref=src, dst_ref=dst, send_sem=send, recv_sem=recv, device_id=device, device_id_type=MESH
    )


def drain(ref, sem):
    pltpu.make_async_copy(ref, ref, sem).wait()


def kernel(
    beams_hbm, basis_hbm, fore_hbm, sig_hbm, start_ref, width_ref, proj_ref, kl_ref,
    beam_v, block_v, fore_v, sig_v, basis_t, basis_in, made, beam_f, basis_f, spec, part, got, half, halves, square,
    term, got5, got6, got7, kl_v, local, send, recv,
):
    w = lax.axis_index("wide")
    n = lax.axis_index("narrow")
    y, q = lax.div(w, 4), lax.rem(w, 4)
    z, x = lax.div(n, 4), lax.rem(n, 4)
    chip, core = lax.div(w, 2), lax.rem(w, 2)
    g = x * 4 + q

    offset = lax.rem(x - lax.rem(chip, 4) + 4, 4)
    gives_basis = (lax.div(chip, 4) == z) & (lax.rem(offset, 2) == 1)
    first = lax.div(offset, 2)
    basis_source = (2 * n + lax.div(y, 4), 4 * z + lax.rem(x + 1 + 2 * lax.rem(y, 2), 4))
    gives_beams = lax.div(n, 2) == y
    own_beam = (x == 0) | (x == 3)

    load_fore = pltpu.make_async_copy(fore_hbm, fore_v, local.at[1])
    load_sig = pltpu.make_async_copy(sig_hbm, sig_v, local.at[2])
    load_beam = pltpu.make_async_copy(beams_hbm.at[y], beam_v, local.at[3])

    def load_block(i):
        row = pl.multiple_of(256 * (first + 2 * i), 256)
        return pltpu.make_async_copy(basis_hbm.at[pl.ds(row, 256), :], block_v.at[i], local.at[4 + i])

    @pl.when(gives_basis)
    def _():
        load_block(0).start()
        load_block(1).start()

    load_fore.start()
    load_sig.start()
    load_beam.start()

    def in_narrow(i):
        other = lax.rem(n + i, 16)
        return other, (w, other)

    def in_group(i):
        other = lax.rem(g + i, 16)
        return other, (y * 4 + lax.rem(other, 4), z * 4 + lax.div(other, 4))

    def in_y(i):
        return (4 * lax.rem(y + i, 8) + q, n)

    def in_q(i):
        return (4 * y + lax.rem(q + i, 4), n)

    barrier = pltpu.get_barrier_semaphore()

    def greet(device):
        pl.semaphore_signal(barrier, inc=1, device_id=device, device_id_type=MESH)

    greet(basis_source)

    @pl.loop(1, 16)
    def _(i):
        greet(in_narrow(i)[1])
        greet(in_group(i)[1])

    @pl.loop(1, 8)
    def _(i):
        greet(in_y(i))

    @pl.when(gives_basis)
    def _():
        for i in range(2):
            load_block(i).wait()
            basis_t[i] = block_v[i].astype(F32).T.astype(BF16)

    load_fore.wait()
    load_sig.wait()
    column = 4 * w + lax.broadcasted_iota(jnp.int32, (4, 256), 0)
    for f in range(8):
        low = start_ref[f]
        inband = ((column >= low) & (column < low + width_ref[f])).astype(F32)
        spec[q, pl.ds(4 * f, 4), :] = fore_v[f] + inband * sig_v[f]

    pl.semaphore_wait(barrier, 37 + 8 * gives_basis.astype(jnp.int32))

    @pl.when(gives_basis)
    def _():
        for i in range(2):
            for r in range(4):
                device = (4 * (4 * core + first + 2 * i) + r, chip)
                put(basis_t.at[i, pl.ds(32 * r, 32), :], basis_in, send.at[1], recv.at[1], device).start()

    for i in range(1, 4):
        put(spec.at[q], spec.at[q], send.at[0], recv.at[0], in_q(i)).start()
    quarter = beam_f.at[pl.ds(pl.multiple_of(64 * q, 64), 64), :]

    @pl.when(gives_beams)
    def _():
        for i in range(8):
            other = 4 * (i // 2) + 2 * lax.rem(n, 2) + i % 2
            source = beams_hbm.at[4 * (i % 2) + i // 2, pl.ds(pl.multiple_of(64 * q, 64), 64), :]

            @pl.when(other == n)
            def _():
                pltpu.make_async_copy(source, quarter, recv.at[2]).start()

            @pl.when(other != n)
            def _():
                put(source, quarter, send.at[2], recv.at[2], (w, other)).start()

    @pl.when(q == x)
    def _():
        source = basis_hbm.at[pl.ds(pl.multiple_of(256 * z, 256), 256), :]
        pltpu.make_async_copy(source, basis_f, recv.at[3]).start()
        for i in range(1, 4):
            put(source, basis_f, send.at[3], recv.at[3], in_q(i)).start()

    load_beam.wait()
    drain(basis_in, recv.at[1])
    made[y] = jnp.dot(basis_in[...], beam_v[...], preferred_element_type=F32).astype(BF16)

    for i in range(1, 8):
        put(made.at[y], made.at[y], send.at[4], recv.at[4], in_y(i)).start()
    drain(quarter, recv.at[2])
    for i in range(1, 4):
        put(quarter, quarter, send.at[5], recv.at[5], in_q(i)).start()
    drain(spec.at[pl.ds(0, 3)], recv.at[0])
    drain(made.at[pl.ds(0, 7)], recv.at[4])

    wide_made = [made[f].astype(F32) for f in range(8)]
    for step in range(4):
        to_z = lax.rem(z + 1 + step, 4)
        for r in range(4):
            total = spec[r, pl.ds(to_z, 1), :] * wide_made[0]
            for f in range(1, 8):
                total = total + spec[r, pl.ds(4 * f + to_z, 1), :] * wide_made[f]
            part[4 * to_z + r] = total.astype(BF16)
        for r in range(4):
            other = 4 * to_z + r

            @pl.when(other != n)
            def _():
                put(part.at[other], got.at[n], send.at[6], recv.at[6], (w, other)).start()

    got[n] = part[n]
    drain(beam_f.at[pl.ds(0, 192), :], recv.at[5])
    drain(basis_f, recv.at[3])
    drain(got.at[pl.ds(0, 15)], recv.at[6])
    total = got[0].astype(F32)
    for i in range(1, 16):
        total = total + got[i].astype(F32)

    high, low = split(total)
    turned = nt(high, beam_f[...]) + nt(low, beam_f[...])
    turned_high, turned_low = split(turned)
    term[...] = jnp.dot(turned_high, basis_f[...], preferred_element_type=F32) + jnp.dot(
        turned_low, basis_f[...], preferred_element_type=F32
    )

    for i in range(1, 4):
        to_x = lax.rem(x + i, 4)
        source = term.at[pl.ds(pl.multiple_of(8 * to_x, 8), 8), :]
        put(source, got5.at[x], send.at[8], recv.at[8], (w, 4 * z + to_x)).start()
    half[0] = turned[:, 0:128]
    half[1] = turned[:, 128:256]
    for to_x in range(4):
        same = (q == x) & (x == to_x)

        @pl.when(same)
        def _():
            pltpu.make_async_copy(half.at[to_x // 2], halves.at[q], recv.at[7]).start()

        @pl.when(jnp.logical_not(same))
        def _():
            put(half.at[to_x // 2], halves.at[q], send.at[7], recv.at[7], (4 * y + x, 4 * z + to_x)).start()

    got5[x] = term[pl.ds(pl.multiple_of(8 * x, 8), 8), :]
    drain(got5.at[pl.ds(0, 3)], recv.at[8])
    got6[z] = (got5[0] + got5[1]) + (got5[2] + got5[3])

    for i in range(1, 4):
        put(got6.at[z], got6.at[z], send.at[9], recv.at[9], (w, 4 * lax.rem(z + i, 4) + x)).start()
    drain(halves, recv.at[7])
    square[...] = halves[...].reshape(128, 128).T
    proj_ref[...] = square[pl.ds(pl.multiple_of(64 * lax.rem(x, 2), 64), 64), :]
    drain(got6.at[pl.ds(0, 3)], recv.at[9])
    got7[y] = (got6[0] + got6[1]) + (got6[2] + got6[3])
    for i in range(1, 8):
        put(got7.at[y], got7.at[y], send.at[10], recv.at[10], in_y(i)).start()
    drain(got7.at[pl.ds(0, 7)], recv.at[10])
    total = got7[0]
    for i in range(1, 8):
        total = total + got7[i]
    here = kl_v.at[pl.ds(pl.multiple_of(32 * q + 8 * x, 8), 8), :]
    here[...] = total * (1.0 / 128)

    @pl.loop(1, 16)
    def _(i):
        other, device = in_group(i)
        put(here, here, send.at[11], recv.at[11], device).start()

    drain(kl_v.at[pl.ds(0, 120)], recv.at[11])
    kl_ref[...] = kl_v[...]

    drain(spec.at[pl.ds(0, 3)], send.at[0])

    @pl.when(gives_basis)
    def _():
        drain(basis_t, send.at[1])

    @pl.when(gives_beams & own_beam)
    def _():
        drain(got.at[pl.ds(0, 14)], send.at[2])

    @pl.when(gives_beams & jnp.logical_not(own_beam))
    def _():
        drain(got, send.at[2])

    @pl.when(q == x)
    def _():
        drain(got.at[pl.ds(0, 12)], send.at[3])

    drain(made.at[pl.ds(0, 7)], send.at[4])
    drain(beam_f.at[pl.ds(0, 192), :], send.at[5])
    drain(got.at[pl.ds(0, 15)], send.at[6])

    @pl.when(q == x)
    def _():
        drain(halves.at[pl.ds(0, 3)], send.at[7])

    @pl.when(q != x)
    def _():
        drain(halves, send.at[7])

    drain(got5.at[pl.ds(0, 3)], send.at[8])
    drain(got6.at[pl.ds(0, 3)], send.at[9])
    drain(got7.at[pl.ds(0, 7)], send.at[10])
    drain(kl_v.at[pl.ds(0, 120)], send.at[11])


def per_device(beams, basis, foreground, signal, band_start, band_width):
    anywhere = pl.BlockSpec(memory_space=pl.ANY)
    scalars = pl.BlockSpec(memory_space=pltpu.SMEM)
    vector = pl.BlockSpec(memory_space=pltpu.VMEM)
    return pl.pallas_call(
        kernel,
        out_shape=(
            jax.ShapeDtypeStruct((64, 128), F32),
            jax.ShapeDtypeStruct((128, 128), F32),
        ),
        in_specs=[anywhere] * 4 + [scalars] * 2,
        out_specs=(vector, vector),
        scratch_shapes=[
            pltpu.VMEM((256, 256), BF16),
            pltpu.VMEM((2, 256, 128), BF16),
            pltpu.VMEM((8, 4, 256), F32),
            pltpu.VMEM((8, 4, 256), F32),
            pltpu.VMEM((2, 128, 256), BF16),
            pltpu.VMEM((32, 256), BF16),
            pltpu.VMEM((8, 32, 256), BF16),
            pltpu.VMEM((256, 256), BF16),
            pltpu.VMEM((256, 128), BF16),
            pltpu.VMEM((4, 32, 256), F32),
            pltpu.VMEM((16, 32, 256), BF16),
            pltpu.VMEM((16, 32, 256), BF16),
            pltpu.VMEM((2, 32, 128), F32),
            pltpu.VMEM((4, 32, 128), F32),
            pltpu.VMEM((128, 128), F32),
            pltpu.VMEM((32, 128), F32),
            pltpu.VMEM((4, 8, 128), F32),
            pltpu.VMEM((4, 8, 128), F32),
            pltpu.VMEM((8, 8, 128), F32),
            pltpu.VMEM((128, 128), F32),
            pltpu.SemaphoreType.DMA((6,)),
            pltpu.SemaphoreType.DMA((12,)),
            pltpu.SemaphoreType.DMA((12,)),
        ],
        compiler_params=pltpu.CompilerParams(
            collective_id=0, has_side_effects=True, vmem_limit_bytes=60 << 20
        ),
    )(beams, basis, foreground, signal, band_start, band_width)


def solution(mesh):
    placed = (
        P("narrow", None, None),
        P("wide", None),
        P("narrow", "wide", None),
        P("narrow", "wide", None),
        P("narrow"),
        P("narrow"),
    )
    return jax.shard_map(
        per_device,
        mesh=mesh,
        in_specs=placed,
        out_specs=(P(("wide", "narrow"), None), P()),
        check_vma=False,
    )
```

```python
import jax
import jax.numpy as jnp
from jax import lax
from jax.experimental import pallas as pl
from jax.experimental.pallas import tpu as pltpu
from jax.sharding import PartitionSpec as P

MESH = pl.DeviceIdType.MESH
F32 = jnp.float32
BF16 = jnp.bfloat16
NT = (((1,), (1,)), ((), ()))


def nt(a, b):
    return lax.dot_general(a, b, NT, preferred_element_type=F32)


def split(value):
    high = value.astype(BF16)
    return high, (value - high.astype(F32)).astype(BF16)


def put(src, dst, send, recv, device):
    return pltpu.make_async_remote_copy(
        src_ref=src, dst_ref=dst, send_sem=send, recv_sem=recv, device_id=device, device_id_type=MESH
    )


def drain(ref, sem):
    pltpu.make_async_copy(ref, ref, sem).wait()


def kernel(
    beams_hbm, basis_hbm, fore_hbm, sig_hbm, start_ref, width_ref, proj_ref, kl_ref,
    beam_v, block_v, fore_v, sig_v, basis_t, basis_in, made, beam_f, basis_f, spec, part, got, half, halves, square,
    term, got5, got6, got7, kl_v, local, send, recv,
):
    w = lax.axis_index("wide")
    n = lax.axis_index("narrow")
    y, q = lax.div(w, 4), lax.rem(w, 4)
    z, x = lax.div(n, 4), lax.rem(n, 4)
    chip, core = lax.div(w, 2), lax.rem(w, 2)
    g = x * 4 + q

    offset = lax.rem(x - lax.rem(chip, 4) + 4, 4)
    gives_basis = (lax.div(chip, 4) == z) & (lax.rem(offset, 2) == 1)
    first = lax.div(offset, 2)
    basis_source = (2 * n + lax.div(y, 4), 4 * z + lax.rem(x + 1 + 2 * lax.rem(y, 2), 4))
    gives_beams = lax.div(n, 2) == y
    own_beam = (x == 0) | (x == 3)

    load_fore = pltpu.make_async_copy(fore_hbm, fore_v, local.at[1])
    load_sig = pltpu.make_async_copy(sig_hbm, sig_v, local.at[2])
    load_beam = pltpu.make_async_copy(beams_hbm.at[y], beam_v, local.at[3])

    def load_block(i):
        row = pl.multiple_of(256 * (first + 2 * i), 256)
        return pltpu.make_async_copy(basis_hbm.at[pl.ds(row, 256), :], block_v.at[i], local.at[4 + i])

    @pl.when(gives_basis)
    def _():
        load_block(0).start()
        load_block(1).start()

    load_fore.start()
    load_sig.start()
    load_beam.start()

    def in_narrow(i):
        other = lax.rem(n + i, 16)
        return other, (w, other)

    def in_group(i):
        other = lax.rem(g + i, 16)
        return other, (y * 4 + lax.rem(other, 4), z * 4 + lax.div(other, 4))

    def in_y(i):
        return (4 * lax.rem(y + i, 8) + q, n)

    def in_q(i):
        return (4 * y + lax.rem(q + i, 4), n)

    barrier = pltpu.get_barrier_semaphore()

    def greet(device):
        pl.semaphore_signal(barrier, inc=1, device_id=device, device_id_type=MESH)

    greet(basis_source)

    @pl.loop(1, 16)
    def _(i):
        greet(in_narrow(i)[1])
        greet(in_group(i)[1])

    @pl.loop(1, 8)
    def _(i):
        greet(in_y(i))

    @pl.when(gives_basis)
    def _():
        for i in range(2):
            load_block(i).wait()
            basis_t[i] = block_v[i].astype(F32).T.astype(BF16)

    load_fore.wait()
    load_sig.wait()
    column = 4 * w + lax.broadcasted_iota(jnp.int32, (4, 256), 0)
    for f in range(8):
        low = start_ref[f]
        inband = ((column >= low) & (column < low + width_ref[f])).astype(F32)
        spec[q, pl.ds(4 * f, 4), :] = fore_v[f] + inband * sig_v[f]

    pl.semaphore_wait(barrier, 37 + 8 * gives_basis.astype(jnp.int32))

    @pl.when(gives_basis)
    def _():
        for i in range(2):
            for r in range(4):
                device = (4 * (4 * core + first + 2 * i) + r, chip)
                put(basis_t.at[i, pl.ds(32 * r, 32), :], basis_in, send.at[1], recv.at[1], device).start()

    for i in range(1, 4):
        put(spec.at[q], spec.at[q], send.at[0], recv.at[0], in_q(i)).start()
    quarter = beam_f.at[pl.ds(pl.multiple_of(64 * q, 64), 64), :]

    @pl.when(gives_beams)
    def _():
        for i in range(8):
            other = 4 * (i // 2) + 2 * lax.rem(n, 2) + i % 2
            source = beams_hbm.at[4 * (i % 2) + i // 2, pl.ds(pl.multiple_of(64 * q, 64), 64), :]

            @pl.when(other == n)
            def _():
                pltpu.make_async_copy(source, quarter, recv.at[2]).start()

            @pl.when(other != n)
            def _():
                put(source, quarter, send.at[2], recv.at[2], (w, other)).start()

    @pl.when(q == x)
    def _():
        source = basis_hbm.at[pl.ds(pl.multiple_of(256 * z, 256), 256), :]
        pltpu.make_async_copy(source, basis_f, recv.at[3]).start()
        for i in range(1, 4):
            put(source, basis_f, send.at[3], recv.at[3], in_q(i)).start()

    load_beam.wait()
    drain(basis_in, recv.at[1])
    made[y] = jnp.dot(basis_in[...], beam_v[...], preferred_element_type=F32).astype(BF16)

    for i in range(1, 8):
        put(made.at[y], made.at[y], send.at[4], recv.at[4], in_y(i)).start()
    drain(quarter, recv.at[2])
    for i in range(1, 4):
        put(quarter, quarter, send.at[5], recv.at[5], in_q(i)).start()
    drain(spec.at[pl.ds(0, 3)], recv.at[0])
    drain(made.at[pl.ds(0, 7)], recv.at[4])

    wide_made = [made[f].astype(F32) for f in range(8)]
    for step in range(4):
        to_z = lax.rem(z + 1 + step, 4)
        for r in range(4):
            total = spec[r, pl.ds(to_z, 1), :] * wide_made[0]
            for f in range(1, 8):
                total = total + spec[r, pl.ds(4 * f + to_z, 1), :] * wide_made[f]
            part[4 * to_z + r] = total.astype(BF16)
        for r in range(4):
            other = 4 * to_z + r

            @pl.when(other != n)
            def _():
                put(part.at[other], got.at[n], send.at[6], recv.at[6], (w, other)).start()

    got[n] = part[n]
    drain(beam_f.at[pl.ds(0, 192), :], recv.at[5])
    drain(basis_f, recv.at[3])
    drain(got.at[pl.ds(0, 15)], recv.at[6])
    total = got[0].astype(F32)
    for i in range(1, 16):
        total = total + got[i].astype(F32)

    high, low = split(total)
    turned = nt(high, beam_f[...]) + nt(low, beam_f[...])
    turned_high, turned_low = split(turned)
    term[...] = jnp.dot(turned_high, basis_f[...], preferred_element_type=F32) + jnp.dot(
        turned_low, basis_f[...], preferred_element_type=F32
    )

    for i in range(1, 4):
        to_x = lax.rem(x + i, 4)
        source = term.at[pl.ds(pl.multiple_of(8 * to_x, 8), 8), :]
        put(source, got5.at[x], send.at[8], recv.at[8], (w, 4 * z + to_x)).start()
    half[0] = turned[:, 0:128]
    half[1] = turned[:, 128:256]
    for to_x in range(4):
        same = (q == x) & (x == to_x)

        @pl.when(same)
        def _():
            pltpu.make_async_copy(half.at[to_x // 2], halves.at[q], recv.at[7]).start()

        @pl.when(jnp.logical_not(same))
        def _():
            put(half.at[to_x // 2], halves.at[q], send.at[7], recv.at[7], (4 * y + x, 4 * z + to_x)).start()

    got5[x] = term[pl.ds(pl.multiple_of(8 * x, 8), 8), :]
    drain(got5.at[pl.ds(0, 3)], recv.at[8])
    got6[z] = (got5[0] + got5[1]) + (got5[2] + got5[3])

    for i in range(1, 4):
        put(got6.at[z], got6.at[z], send.at[9], recv.at[9], (w, 4 * lax.rem(z + i, 4) + x)).start()
    drain(halves, recv.at[7])
    square[...] = halves[...].reshape(128, 128).T
    proj_ref[...] = square[pl.ds(pl.multiple_of(64 * lax.rem(x, 2), 64), 64), :]
    drain(got6.at[pl.ds(0, 3)], recv.at[9])
    got7[y] = (got6[0] + got6[1]) + (got6[2] + got6[3])
    for i in range(1, 8):
        put(got7.at[y], got7.at[y], send.at[10], recv.at[10], in_y(i)).start()
    drain(got7.at[pl.ds(0, 7)], recv.at[10])
    total = got7[0]
    for i in range(1, 8):
        total = total + got7[i]
    here = kl_v.at[pl.ds(pl.multiple_of(32 * q + 8 * x, 8), 8), :]
    here[...] = total * (1.0 / 128)

    @pl.loop(1, 16)
    def _(i):
        other, device = in_group(i)
        put(here, here, send.at[11], recv.at[11], device).start()

    drain(kl_v.at[pl.ds(0, 120)], recv.at[11])
    kl_ref[...] = kl_v[...]

    drain(spec.at[pl.ds(0, 3)], send.at[0])

    @pl.when(gives_basis)
    def _():
        drain(basis_t, send.at[1])

    @pl.when(gives_beams & own_beam)
    def _():
        drain(got.at[pl.ds(0, 14)], send.at[2])

    @pl.when(gives_beams & jnp.logical_not(own_beam))
    def _():
        drain(got, send.at[2])

    @pl.when(q == x)
    def _():
        drain(got.at[pl.ds(0, 12)], send.at[3])

    drain(made.at[pl.ds(0, 7)], send.at[4])
    drain(beam_f.at[pl.ds(0, 192), :], send.at[5])
    drain(got.at[pl.ds(0, 15)], send.at[6])

    @pl.when(q == x)
    def _():
        drain(halves.at[pl.ds(0, 3)], send.at[7])

    @pl.when(q != x)
    def _():
        drain(halves, send.at[7])

    drain(got5.at[pl.ds(0, 3)], send.at[8])
    drain(got6.at[pl.ds(0, 3)], send.at[9])
    drain(got7.at[pl.ds(0, 7)], send.at[10])
    drain(kl_v.at[pl.ds(0, 120)], send.at[11])


def per_device(beams, basis, foreground, signal, band_start, band_width):
    anywhere = pl.BlockSpec(memory_space=pl.ANY)
    scalars = pl.BlockSpec(memory_space=pltpu.SMEM)
    vector = pl.BlockSpec(memory_space=pltpu.VMEM)
    return pl.pallas_call(
        kernel,
        out_shape=(
            pltpu.VMEM((64, 128), F32),
            pltpu.VMEM((128, 128), F32),
        ),
        in_specs=[anywhere] * 4 + [scalars] * 2,
        out_specs=(vector, vector),
        scratch_shapes=[
            pltpu.VMEM((256, 256), BF16),
            pltpu.VMEM((2, 256, 128), BF16),
            pltpu.VMEM((8, 4, 256), F32),
            pltpu.VMEM((8, 4, 256), F32),
            pltpu.VMEM((2, 128, 256), BF16),
            pltpu.VMEM((32, 256), BF16),
            pltpu.VMEM((8, 32, 256), BF16),
            pltpu.VMEM((256, 256), BF16),
            pltpu.VMEM((256, 128), BF16),
            pltpu.VMEM((4, 32, 256), F32),
            pltpu.VMEM((16, 32, 256), BF16),
            pltpu.VMEM((16, 32, 256), BF16),
            pltpu.VMEM((2, 32, 128), F32),
            pltpu.VMEM((4, 32, 128), F32),
            pltpu.VMEM((128, 128), F32),
            pltpu.VMEM((32, 128), F32),
            pltpu.VMEM((4, 8, 128), F32),
            pltpu.VMEM((4, 8, 128), F32),
            pltpu.VMEM((8, 8, 128), F32),
            pltpu.VMEM((128, 128), F32),
            pltpu.SemaphoreType.DMA((6,)),
            pltpu.SemaphoreType.DMA((12,)),
            pltpu.SemaphoreType.DMA((12,)),
        ],
        compiler_params=pltpu.CompilerParams(
            collective_id=0, has_side_effects=True, vmem_limit_bytes=60 << 20
        ),
    )(beams, basis, foreground, signal, band_start, band_width)


def solution(mesh):
    placed = (
        P("narrow", None, None),
        P("wide", None),
        P("narrow", "wide", None),
        P("narrow", "wide", None),
        P("narrow"),
        P("narrow"),
    )
    return jax.shard_map(
        per_device,
        mesh=mesh,
        in_specs=placed,
        out_specs=(P(("wide", "narrow"), None), P()),
        check_vma=False,
    )
```

```python
import jax
import jax.numpy as jnp
from jax import lax
from jax.experimental import pallas as pl
from jax.experimental.pallas import tpu as pltpu
from jax.sharding import PartitionSpec as P

MESH = pl.DeviceIdType.MESH
F32 = jnp.float32
BF16 = jnp.bfloat16
NT = (((1,), (1,)), ((), ()))


def nt(a, b):
    return lax.dot_general(a, b, NT, preferred_element_type=F32)


def split(value):
    high = value.astype(BF16)
    return high, (value - high.astype(F32)).astype(BF16)


def put(src, dst, send, recv, device):
    return pltpu.make_async_remote_copy(
        src_ref=src, dst_ref=dst, send_sem=send, recv_sem=recv, device_id=device, device_id_type=MESH
    )


def drain(ref, sem):
    pltpu.make_async_copy(ref, ref, sem).wait()


def kernel(
    beams_hbm, basis_hbm, fore_hbm, sig_hbm, start_ref, width_ref, proj_ref, kl_ref,
    beam_v, block_v, fore_v, sig_v, basis_t, basis_in, made, pieces, wide, beam_f, basis_f, flipped, beam_in, prod, spec, part,
    got, mine, rows, got6, got7, kl_v, local, send, recv,
):
    w = lax.axis_index("wide")
    n = lax.axis_index("narrow")
    y, q = lax.div(w, 4), lax.rem(w, 4)
    z, x = lax.div(n, 4), lax.rem(n, 4)
    chip, core = lax.div(w, 2), lax.rem(w, 2)
    g = x * 4 + q

    offset = lax.rem(x - lax.rem(chip, 4) + 4, 4)
    gives_basis = (lax.div(chip, 4) == z) & (lax.rem(offset, 2) == 1)
    first = lax.div(offset, 2)
    basis_source = (2 * n + lax.div(y, 4), 4 * z + lax.rem(x + 1 + 2 * lax.rem(y, 2), 4))
    gives_beams = lax.div(n, 2) == y
    own_beam = (x == 0) | (x == 3)
    beam_source = 2 * y + lax.div(x, 2)

    load_fore = pltpu.make_async_copy(fore_hbm, fore_v, local.at[1])
    load_sig = pltpu.make_async_copy(sig_hbm, sig_v, local.at[2])
    load_beam = pltpu.make_async_copy(beams_hbm.at[y], beam_v, local.at[3])

    def load_block(i):
        row = pl.multiple_of(256 * (first + 2 * i), 256)
        return pltpu.make_async_copy(basis_hbm.at[pl.ds(row, 256), :], block_v.at[i], local.at[4 + i])

    @pl.when(gives_basis)
    def _():
        load_block(0).start()
        load_block(1).start()

    load_fore.start()
    load_sig.start()
    load_beam.start()

    def in_plane(i):
        other = lax.rem(4 * y + x + i, 32)
        return lax.rem(other, 4), (4 * lax.div(other, 4) + q, 4 * z + lax.rem(other, 4))

    def in_group(i):
        other = lax.rem(g + i, 16)
        return other, (y * 4 + lax.rem(other, 4), z * 4 + lax.div(other, 4))

    def in_y(i):
        return (4 * lax.rem(y + i, 8) + q, n)

    def in_z(i):
        return (w, 4 * lax.rem(z + i, 4) + x)

    def in_q(i):
        return (4 * y + lax.rem(q + i, 4), n)

    barrier = pltpu.get_barrier_semaphore()

    def greet(device):
        pl.semaphore_signal(barrier, inc=1, device_id=device, device_id_type=MESH)

    greet(basis_source)

    @pl.when(beam_source != n)
    def _():
        greet((w, beam_source))

    @pl.loop(1, 16)
    def _(i):
        greet(in_group(i)[1])

    @pl.loop(1, 32)
    def _(i):
        greet(in_plane(i)[1])

    for i in range(1, 4):
        greet(in_z(i))

    @pl.when(gives_basis)
    def _():
        for i in range(2):
            load_block(i).wait()
            basis_t[i] = block_v[i].astype(F32).T.astype(BF16)

    load_fore.wait()
    load_sig.wait()
    column = 4 * w + lax.broadcasted_iota(jnp.int32, (4, 256), 0)
    for f in range(8):
        low = start_ref[f]
        inband = ((column >= low) & (column < low + width_ref[f])).astype(F32)
        spec[g, pl.ds(4 * f, 4), :] = fore_v[f] + inband * sig_v[f]

    expected = 8 * gives_basis.astype(jnp.int32) + gives_beams.astype(jnp.int32) * (8 - own_beam.astype(jnp.int32))
    pl.semaphore_wait(barrier, 49 + expected)

    @pl.when(gives_basis)
    def _():
        for i in range(2):
            for r in range(4):
                device = (4 * (4 * core + first + 2 * i) + r, chip)
                put(basis_t.at[i, pl.ds(32 * r, 32), :], basis_in, send.at[1], recv.at[1], device).start()

    @pl.loop(1, 16)
    def _(i):
        put(spec.at[g], spec.at[g], send.at[0], recv.at[0], in_group(i)[1]).start()

    quarter = beam_f.at[pl.ds(pl.multiple_of(64 * q, 64), 64), :]

    @pl.when(gives_beams)
    def _():
        for i in range(8):
            other = 4 * (i // 2) + 2 * lax.rem(n, 2) + i % 2
            source = beams_hbm.at[4 * (i % 2) + i // 2, pl.ds(pl.multiple_of(64 * q, 64), 64), :]

            @pl.when(other == n)
            def _():
                pltpu.make_async_copy(source, quarter, recv.at[2]).start()

            @pl.when(other != n)
            def _():
                put(source, quarter, send.at[12], recv.at[2], (w, other)).start()

    @pl.when(q == x)
    def _():
        source = basis_hbm.at[pl.ds(pl.multiple_of(256 * z, 256), 256), :]
        pltpu.make_async_copy(source, basis_f, recv.at[3]).start()
        for i in range(1, 4):
            put(source, basis_f, send.at[3], recv.at[3], in_q(i)).start()

    load_beam.wait()
    drain(basis_in, recv.at[1])
    product = jnp.dot(basis_in[...], beam_v[...], preferred_element_type=F32)
    for r in range(4):
        made[r] = product[8 * r : 8 * r + 8].astype(BF16)

    me = 8 * x + y

    @pl.loop(1, 32)
    def _(i):
        to_x, device = in_plane(i)
        put(made.at[to_x], pieces.at[me], send.at[4], recv.at[4], device).start()

    pieces[me] = made[x]

    drain(quarter, recv.at[2])
    for i in range(1, 4):
        put(quarter, quarter, send.at[5], recv.at[5], in_q(i)).start()

    @pl.when(q == x)
    def _():
        pltpu.make_async_copy(quarter, beam_in, recv.at[7]).start()

    @pl.when(q != x)
    def _():
        put(quarter, beam_in, send.at[7], recv.at[7], (4 * y + x, 4 * z + q)).start()

    drain(basis_f, recv.at[3])
    lanes = pl.ds(pl.multiple_of(32 * q, 32), 32)
    drain(beam_f.at[pl.ds(0, 192), :], recv.at[5])
    flipped[...] = basis_f[...].astype(F32).T
    prod[g] = jnp.dot(flipped[lanes, :].astype(BF16), beam_f[...], preferred_element_type=F32).astype(BF16)

    drain(spec.at[pl.ds(0, 15)], recv.at[0])
    drain(pieces.at[pl.ds(0, 31)], recv.at[4])

    for i in range(32):
        wide[i] = pieces[i].astype(F32)
    for step in (2, 1, 3, 0):
        to_z = lax.rem(z + step, 4)
        for r in range(4):
            total = None
            for xx in range(4):
                for f in range(8):
                    item = spec[4 * xx + r, pl.ds(4 * f + to_z, 1), :] * wide[8 * xx + f]
                    total = item if total is None else total + item
            part[to_z, r] = total.astype(BF16)
        if step:
            put(part.at[to_z], got.at[z], send.at[6], recv.at[6], (w, 4 * to_z + x)).start()

    @pl.loop(1, 16)
    def _(i):
        put(prod.at[g], prod.at[g], send.at[2], recv.at[11], in_group(i)[1]).start()

    got[z] = part[z]
    drain(got.at[pl.ds(0, 3)], recv.at[6])
    drain(prod.at[pl.ds(0, 15)], recv.at[11])

    term = None
    for r in range(4):
        total = (got[0, r].astype(F32) + got[1, r].astype(F32)) + (got[2, r].astype(F32) + got[3, r].astype(F32))
        mine[r] = total
        high, low = split(total)
        for part_of in (high, low):
            item = jnp.concatenate([nt(part_of, prod[4 * r + c]) for c in range(4)], axis=1)
            term = item if term is None else term + item
    got6[z] = term

    for i in range(1, 4):
        put(got6.at[z], got6.at[z], send.at[9], recv.at[9], in_z(i)).start()

    place = pl.multiple_of(32 * q + 8 * x, 8)

    @pl.loop(1, 16)
    def _(i):
        other, device = in_group(i)
        put(mine.at[lax.rem(other, 4)], rows.at[pl.ds(place, 8), :], send.at[8], recv.at[8], device).start()

    rows[pl.ds(place, 8), :] = mine[q]
    drain(got6.at[pl.ds(0, 3)], recv.at[9])
    got7[y] = (got6[0] + got6[1]) + (got6[2] + got6[3])
    for i in range(1, 8):
        put(got7.at[y], got7.at[y], send.at[10], recv.at[10], in_y(i)).start()
    drain(beam_in, recv.at[7])
    drain(rows.at[pl.ds(0, 120)], recv.at[8])
    high, low = split(rows[...])
    chunk = beam_in[...]
    proj_ref[...] = nt(chunk, high) + nt(chunk, low)
    drain(got7.at[pl.ds(0, 7)], recv.at[10])
    total = got7[0]
    for i in range(1, 8):
        total = total + got7[i]
    here = kl_v.at[pl.ds(place, 8), :]
    here[...] = total * (1.0 / 128)

    @pl.loop(1, 16)
    def _(i):
        put(here, here, send.at[11], recv.at[12], in_group(i)[1]).start()

    drain(kl_v.at[pl.ds(0, 120)], recv.at[12])
    kl_ref[...] = kl_v[...]

    drain(spec.at[pl.ds(0, 15)], send.at[0])

    @pl.when(gives_basis)
    def _():
        drain(basis_t, send.at[1])

    @pl.when(gives_beams & own_beam)
    def _():
        drain(prod.at[pl.ds(0, 14)], send.at[12])

    @pl.when(gives_beams & jnp.logical_not(own_beam))
    def _():
        drain(prod, send.at[12])

    @pl.when(q == x)
    def _():
        drain(prod.at[pl.ds(0, 12)], send.at[3])

    @pl.when(q != x)
    def _():
        drain(beam_in, send.at[7])

    drain(prod.at[pl.ds(0, 15)], send.at[2])
    drain(pieces.at[pl.ds(0, 31)], send.at[4])
    drain(beam_f.at[pl.ds(0, 192), :], send.at[5])
    drain(got.at[pl.ds(0, 3)], send.at[6])
    drain(rows.at[pl.ds(0, 120)], send.at[8])
    drain(got6.at[pl.ds(0, 3)], send.at[9])
    drain(got7.at[pl.ds(0, 7)], send.at[10])
    drain(kl_v.at[pl.ds(0, 120)], send.at[11])


def per_device(beams, basis, foreground, signal, band_start, band_width):
    anywhere = pl.BlockSpec(memory_space=pl.ANY)
    scalars = pl.BlockSpec(memory_space=pltpu.SMEM)
    vector = pl.BlockSpec(memory_space=pltpu.VMEM)
    return pl.pallas_call(
        kernel,
        out_shape=(
            pltpu.VMEM((64, 128), F32),
            pltpu.VMEM((128, 128), F32),
        ),
        in_specs=[anywhere] * 4 + [scalars] * 2,
        out_specs=(vector, vector),
        scratch_shapes=[
            pltpu.VMEM((256, 256), BF16),
            pltpu.VMEM((2, 256, 128), BF16),
            pltpu.VMEM((8, 4, 256), F32),
            pltpu.VMEM((8, 4, 256), F32),
            pltpu.VMEM((2, 128, 256), BF16),
            pltpu.VMEM((32, 256), BF16),
            pltpu.VMEM((4, 8, 256), BF16),
            pltpu.VMEM((32, 8, 256), BF16),
            pltpu.VMEM((32, 8, 256), F32),
            pltpu.VMEM((256, 256), BF16),
            pltpu.VMEM((256, 128), BF16),
            pltpu.VMEM((128, 256), F32),
            pltpu.VMEM((64, 256), BF16),
            pltpu.VMEM((16, 32, 256), BF16),
            pltpu.VMEM((16, 32, 256), F32),
            pltpu.VMEM((4, 4, 8, 256), BF16),
            pltpu.VMEM((4, 4, 8, 256), BF16),
            pltpu.VMEM((4, 8, 256), F32),
            pltpu.VMEM((128, 256), F32),
            pltpu.VMEM((4, 8, 128), F32),
            pltpu.VMEM((8, 8, 128), F32),
            pltpu.VMEM((128, 128), F32),
            pltpu.SemaphoreType.DMA((6,)),
            pltpu.SemaphoreType.DMA((13,)),
            pltpu.SemaphoreType.DMA((13,)),
        ],
        compiler_params=pltpu.CompilerParams(
            collective_id=0, has_side_effects=True, vmem_limit_bytes=60 << 20
        ),
    )(beams, basis, foreground, signal, band_start, band_width)


def solution(mesh):
    placed = (
        P("narrow", None, None),
        P("wide", None),
        P("narrow", "wide", None),
        P("narrow", "wide", None),
        P("narrow"),
        P("narrow"),
    )
    return jax.shard_map(
        per_device,
        mesh=mesh,
        in_specs=placed,
        out_specs=(P(("wide", "narrow"), None), P()),
        check_vma=False,
    )
```

```python
import jax
import jax.numpy as jnp
from jax import lax
from jax.experimental import pallas as pl
from jax.experimental.pallas import tpu as pltpu
from jax.sharding import PartitionSpec as P

MESH = pl.DeviceIdType.MESH
F32 = jnp.float32
BF16 = jnp.bfloat16
NT = (((1,), (1,)), ((), ()))


def nt(a, b):
    return lax.dot_general(a, b, NT, preferred_element_type=F32)


def split(value):
    high = value.astype(BF16)
    return high, (value - high.astype(F32)).astype(BF16)


def put(src, dst, send, recv, device):
    return pltpu.make_async_remote_copy(
        src_ref=src, dst_ref=dst, send_sem=send, recv_sem=recv, device_id=device, device_id_type=MESH
    )


def drain(ref, sem):
    pltpu.make_async_copy(ref, ref, sem).wait()


def kernel(
    beams_hbm, basis_hbm, fore_hbm, sig_hbm, start_ref, width_ref, proj_ref, kl_ref,
    beam_v, block_v, fore_v, sig_v, basis_t, basis_in, made, pieces, wide, beam_f, basis_f, flipped, beam_in, prod, spec, part,
    got, mine, rows, got6, got7, kl_v, local, send, recv,
):
    w = lax.axis_index("wide")
    n = lax.axis_index("narrow")
    y, q = lax.div(w, 4), lax.rem(w, 4)
    z, x = lax.div(n, 4), lax.rem(n, 4)
    chip, core = lax.div(w, 2), lax.rem(w, 2)
    g = x * 4 + q
    pair = 2 * x + lax.div(q, 2)
    own = 8 * core + pair
    sibling = (w + 1 - 2 * core, n)

    offset = lax.rem(x - lax.rem(chip, 4) + 4, 4)
    gives_basis = (lax.div(chip, 4) == z) & (lax.rem(offset, 2) == 1)
    first = lax.div(offset, 2)
    basis_source = (2 * n + lax.div(y, 4), 4 * z + lax.rem(x + 1 + 2 * lax.rem(y, 2), 4))
    gives_beams = lax.div(n, 2) == y
    own_beam = (x == 0) | (x == 3)
    beam_source = 2 * y + lax.div(x, 2)

    load_fore = pltpu.make_async_copy(fore_hbm, fore_v, local.at[1])
    load_sig = pltpu.make_async_copy(sig_hbm, sig_v, local.at[2])
    load_beam = pltpu.make_async_copy(beams_hbm.at[y], beam_v, local.at[3])

    def load_block(i):
        row = pl.multiple_of(256 * (first + 2 * i), 256)
        return pltpu.make_async_copy(basis_hbm.at[pl.ds(row, 256), :], block_v.at[i], local.at[4 + i])

    @pl.when(gives_basis)
    def _():
        load_block(0).start()
        load_block(1).start()

    load_fore.start()
    load_sig.start()
    load_beam.start()

    def in_plane(i):
        other = lax.rem(4 * y + x + i, 32)
        return lax.rem(other, 4), (4 * lax.div(other, 4) + q, 4 * z + lax.rem(other, 4))

    def in_group(i):
        other = lax.rem(g + i, 16)
        return other, (y * 4 + lax.rem(other, 4), z * 4 + lax.div(other, 4))

    def in_core(i):
        other = lax.rem(pair + i, 8)
        return (4 * y + 2 * lax.rem(other, 2) + core, 4 * z + lax.div(other, 2))

    def in_y(i):
        return (4 * lax.rem(y + i, 8) + q, n)

    def in_z(i):
        return (w, 4 * lax.rem(z + i, 4) + x)

    def in_q(i):
        return (4 * y + lax.rem(q + i, 4), n)

    barrier = pltpu.get_barrier_semaphore()

    def greet(device):
        pl.semaphore_signal(barrier, inc=1, device_id=device, device_id_type=MESH)

    greet(basis_source)

    @pl.when(beam_source != n)
    def _():
        greet((w, beam_source))

    @pl.loop(1, 16)
    def _(i):
        greet(in_group(i)[1])

    @pl.loop(1, 32)
    def _(i):
        greet(in_plane(i)[1])

    for i in range(1, 4):
        greet(in_z(i))

    @pl.when(gives_basis)
    def _():
        for i in range(2):
            load_block(i).wait()
            basis_t[i] = block_v[i].astype(F32).T.astype(BF16)

    load_fore.wait()
    load_sig.wait()
    column = 4 * w + lax.broadcasted_iota(jnp.int32, (4, 256), 0)
    for f in range(8):
        low = start_ref[f]
        inband = ((column >= low) & (column < low + width_ref[f])).astype(F32)
        spec[own, pl.ds(4 * f, 4), :] = fore_v[f] + inband * sig_v[f]

    expected = 8 * gives_basis.astype(jnp.int32) + gives_beams.astype(jnp.int32) * (8 - own_beam.astype(jnp.int32))
    pl.semaphore_wait(barrier, 49 + expected)

    @pl.when(gives_basis)
    def _():
        for i in range(2):
            for r in range(4):
                device = (4 * (4 * core + first + 2 * i) + r, chip)
                put(basis_t.at[i, pl.ds(32 * r, 32), :], basis_in, send.at[1], recv.at[1], device).start()

    @pl.loop(1, 8)
    def _(i):
        put(spec.at[own], spec.at[own], send.at[0], recv.at[0], in_core(i)).start()

    quarter = beam_f.at[pl.ds(pl.multiple_of(64 * q, 64), 64), :]

    @pl.when(gives_beams)
    def _():
        for i in range(8):
            other = 4 * (i // 2) + 2 * lax.rem(n, 2) + i % 2
            source = beams_hbm.at[4 * (i % 2) + i // 2, pl.ds(pl.multiple_of(64 * q, 64), 64), :]

            @pl.when(other == n)
            def _():
                pltpu.make_async_copy(source, quarter, recv.at[2]).start()

            @pl.when(other != n)
            def _():
                put(source, quarter, send.at[12], recv.at[2], (w, other)).start()

    @pl.when(q == x)
    def _():
        source = basis_hbm.at[pl.ds(pl.multiple_of(256 * z, 256), 256), :]
        pltpu.make_async_copy(source, basis_f, recv.at[3]).start()
        for i in range(1, 4):
            put(source, basis_f, send.at[3], recv.at[3], in_q(i)).start()

    load_beam.wait()
    drain(basis_in, recv.at[1])
    product = jnp.dot(basis_in[...], beam_v[...], preferred_element_type=F32)
    for r in range(4):
        made[r] = product[8 * r : 8 * r + 8].astype(BF16)

    me = 8 * x + y

    @pl.loop(1, 32)
    def _(i):
        to_x, device = in_plane(i)
        put(made.at[to_x], pieces.at[me], send.at[4], recv.at[4], device).start()

    pieces[me] = made[x]

    drain(spec.at[pl.ds(0, 7)], recv.at[0])
    ours = spec.at[pl.ds(pl.multiple_of(8 * core, 8), 8)]
    put(ours, ours, send.at[13], recv.at[13], sibling).start()

    drain(quarter, recv.at[2])
    for i in range(1, 4):
        put(quarter, quarter, send.at[5], recv.at[5], in_q(i)).start()

    @pl.when(q == x)
    def _():
        pltpu.make_async_copy(quarter, beam_in, recv.at[7]).start()

    @pl.when(q != x)
    def _():
        put(quarter, beam_in, send.at[7], recv.at[7], (4 * y + x, 4 * z + q)).start()

    drain(spec.at[pl.ds(0, 8)], recv.at[13])
    drain(pieces.at[pl.ds(0, 31)], recv.at[4])

    for i in range(32):
        wide[i] = pieces[i].astype(F32)
    for step in (2, 1, 3, 0):
        to_z = lax.rem(z + step, 4)
        for r in range(4):
            total = None
            for xx in range(4):
                for f in range(8):
                    item = spec[8 * (r % 2) + 2 * xx + r // 2, pl.ds(4 * f + to_z, 1), :] * wide[8 * xx + f]
                    total = item if total is None else total + item
            part[to_z, r] = total.astype(BF16)
        if step:
            put(part.at[to_z], got.at[z], send.at[6], recv.at[6], (w, 4 * to_z + x)).start()

    drain(basis_f, recv.at[3])
    lanes = pl.ds(pl.multiple_of(32 * q, 32), 32)
    drain(beam_f.at[pl.ds(0, 192), :], recv.at[5])
    flipped[...] = basis_f[...].astype(F32).T
    prod[own] = jnp.dot(flipped[lanes, :].astype(BF16), beam_f[...], preferred_element_type=F32).astype(BF16)

    @pl.loop(1, 8)
    def _(i):
        put(prod.at[own], prod.at[own], send.at[2], recv.at[11], in_core(i)).start()

    got[z] = part[z]
    drain(prod.at[pl.ds(0, 7)], recv.at[11])
    shared = prod.at[pl.ds(pl.multiple_of(8 * core, 8), 8)]
    put(shared, shared, send.at[14], recv.at[14], sibling).start()
    drain(got.at[pl.ds(0, 3)], recv.at[6])
    drain(prod.at[pl.ds(0, 8)], recv.at[14])

    term = None
    for r in range(4):
        total = (got[0, r].astype(F32) + got[1, r].astype(F32)) + (got[2, r].astype(F32) + got[3, r].astype(F32))
        mine[r] = total
        high, low = split(total)
        for part_of in (high, low):
            item = jnp.concatenate([nt(part_of, prod[8 * (c % 2) + 2 * r + c // 2]) for c in range(4)], axis=1)
            term = item if term is None else term + item
    got6[z] = term

    for i in range(1, 4):
        put(got6.at[z], got6.at[z], send.at[9], recv.at[9], in_z(i)).start()

    place = pl.multiple_of(32 * q + 8 * x, 8)

    @pl.loop(1, 16)
    def _(i):
        other, device = in_group(i)
        put(mine.at[lax.rem(other, 4)], rows.at[pl.ds(place, 8), :], send.at[8], recv.at[8], device).start()

    rows[pl.ds(place, 8), :] = mine[q]
    drain(got6.at[pl.ds(0, 3)], recv.at[9])
    got7[y] = (got6[0] + got6[1]) + (got6[2] + got6[3])
    for i in range(1, 8):
        put(got7.at[y], got7.at[y], send.at[10], recv.at[10], in_y(i)).start()
    drain(beam_in, recv.at[7])
    drain(rows.at[pl.ds(0, 120)], recv.at[8])
    high, low = split(rows[...])
    chunk = beam_in[...]
    proj_ref[...] = nt(chunk, high) + nt(chunk, low)
    drain(got7.at[pl.ds(0, 7)], recv.at[10])
    total = got7[0]
    for i in range(1, 8):
        total = total + got7[i]
    here = kl_v.at[pl.ds(place, 8), :]
    here[...] = total * (1.0 / 128)

    @pl.loop(1, 16)
    def _(i):
        put(here, here, send.at[11], recv.at[12], in_group(i)[1]).start()

    drain(kl_v.at[pl.ds(0, 120)], recv.at[12])
    kl_ref[...] = kl_v[...]

    drain(spec.at[pl.ds(0, 7)], send.at[0])
    drain(spec.at[pl.ds(0, 8)], send.at[13])

    @pl.when(gives_basis)
    def _():
        drain(basis_t, send.at[1])

    @pl.when(gives_beams & own_beam)
    def _():
        drain(prod.at[pl.ds(0, 14)], send.at[12])

    @pl.when(gives_beams & jnp.logical_not(own_beam))
    def _():
        drain(prod, send.at[12])

    @pl.when(q == x)
    def _():
        drain(prod.at[pl.ds(0, 12)], send.at[3])

    @pl.when(q != x)
    def _():
        drain(beam_in, send.at[7])

    drain(prod.at[pl.ds(0, 7)], send.at[2])
    drain(prod.at[pl.ds(0, 8)], send.at[14])
    drain(pieces.at[pl.ds(0, 31)], send.at[4])
    drain(beam_f.at[pl.ds(0, 192), :], send.at[5])
    drain(got.at[pl.ds(0, 3)], send.at[6])
    drain(rows.at[pl.ds(0, 120)], send.at[8])
    drain(got6.at[pl.ds(0, 3)], send.at[9])
    drain(got7.at[pl.ds(0, 7)], send.at[10])
    drain(kl_v.at[pl.ds(0, 120)], send.at[11])


def per_device(beams, basis, foreground, signal, band_start, band_width):
    anywhere = pl.BlockSpec(memory_space=pl.ANY)
    scalars = pl.BlockSpec(memory_space=pltpu.SMEM)
    vector = pl.BlockSpec(memory_space=pltpu.VMEM)
    return pl.pallas_call(
        kernel,
        out_shape=(
            pltpu.VMEM((64, 128), F32),
            pltpu.VMEM((128, 128), F32),
        ),
        in_specs=[anywhere] * 4 + [scalars] * 2,
        out_specs=(vector, vector),
        scratch_shapes=[
            pltpu.VMEM((256, 256), BF16),
            pltpu.VMEM((2, 256, 128), BF16),
            pltpu.VMEM((8, 4, 256), F32),
            pltpu.VMEM((8, 4, 256), F32),
            pltpu.VMEM((2, 128, 256), BF16),
            pltpu.VMEM((32, 256), BF16),
            pltpu.VMEM((4, 8, 256), BF16),
            pltpu.VMEM((32, 8, 256), BF16),
            pltpu.VMEM((32, 8, 256), F32),
            pltpu.VMEM((256, 256), BF16),
            pltpu.VMEM((256, 128), BF16),
            pltpu.VMEM((128, 256), F32),
            pltpu.VMEM((64, 256), BF16),
            pltpu.VMEM((16, 32, 256), BF16),
            pltpu.VMEM((16, 32, 256), F32),
            pltpu.VMEM((4, 4, 8, 256), BF16),
            pltpu.VMEM((4, 4, 8, 256), BF16),
            pltpu.VMEM((4, 8, 256), F32),
            pltpu.VMEM((128, 256), F32),
            pltpu.VMEM((4, 8, 128), F32),
            pltpu.VMEM((8, 8, 128), F32),
            pltpu.VMEM((128, 128), F32),
            pltpu.SemaphoreType.DMA((6,)),
            pltpu.SemaphoreType.DMA((15,)),
            pltpu.SemaphoreType.DMA((15,)),
        ],
        compiler_params=pltpu.CompilerParams(
            collective_id=0, has_side_effects=True, vmem_limit_bytes=60 << 20
        ),
    )(beams, basis, foreground, signal, band_start, band_width)


def solution(mesh):
    placed = (
        P("narrow", None, None),
        P("wide", None),
        P("narrow", "wide", None),
        P("narrow", "wide", None),
        P("narrow"),
        P("narrow"),
    )
    return jax.shard_map(
        per_device,
        mesh=mesh,
        in_specs=placed,
        out_specs=(P(("wide", "narrow"), None), P()),
        check_vma=False,
    )
```

```python
import jax
import jax.numpy as jnp
from jax import lax
from jax.experimental import pallas as pl
from jax.experimental.pallas import tpu as pltpu
from jax.sharding import PartitionSpec as P

MESH = pl.DeviceIdType.MESH
F32 = jnp.float32
BF16 = jnp.bfloat16
NT = (((1,), (1,)), ((), ()))


def nt(a, b):
    return lax.dot_general(a, b, NT, preferred_element_type=F32)


def split(value):
    high = value.astype(BF16)
    return high, (value - high.astype(F32)).astype(BF16)


def put(src, dst, send, recv, device):
    return pltpu.make_async_remote_copy(
        src_ref=src, dst_ref=dst, send_sem=send, recv_sem=recv, device_id=device, device_id_type=MESH
    )


def drain(ref, sem):
    pltpu.make_async_copy(ref, ref, sem).wait()


def kernel(
    beams_hbm, basis_hbm, fore_hbm, sig_hbm, start_ref, width_ref, proj_ref, kl_ref,
    beam_v, block_v, fore_v, sig_v, basis_t, basis_in, made, pieces, wide, beam_f, basis_f, flipped, beam_in, prod, spec, part,
    got, mine, rows, got6, got7, kl_v, local, send, recv,
):
    w = lax.axis_index("wide")
    n = lax.axis_index("narrow")
    y, q = lax.div(w, 4), lax.rem(w, 4)
    z, x = lax.div(n, 4), lax.rem(n, 4)
    chip, core = lax.div(w, 2), lax.rem(w, 2)
    g = x * 4 + q
    pair = 2 * x + lax.div(q, 2)
    own = 8 * core + pair
    sibling = (w + 1 - 2 * core, n)

    gives_basis = chip == n
    basis_source = 2 * n + lax.div(y, 4)
    own_basis = basis_source == w
    gives_beams = lax.div(n, 2) == y
    own_beam = (x == 0) | (x == 3)
    beam_source = 2 * y + lax.div(x, 2)

    load_fore = pltpu.make_async_copy(fore_hbm, fore_v, local.at[1])
    load_sig = pltpu.make_async_copy(sig_hbm, sig_v, local.at[2])
    load_beam = pltpu.make_async_copy(beams_hbm.at[y], beam_v, local.at[3])

    def load_block(i):
        return pltpu.make_async_copy(basis_hbm.at[pl.ds(256 * i, 256), :], block_v.at[i], local.at[4 + i])

    @pl.when(gives_basis)
    def _():
        for i in range(4):
            load_block(i).start()

    load_fore.start()
    load_sig.start()
    load_beam.start()

    ys = [lax.rem(y + i, 8) for i in range(8)]
    xs = [lax.rem(x + i, 4) for i in range(4)]
    zs = [lax.rem(z + i, 4) for i in range(4)]
    qs = [lax.rem(q + i, 4) for i in range(4)]
    half_q = lax.div(q, 2)
    y_rows = [4 * other + q for other in ys]
    x_columns = [4 * z + other for other in xs]
    q_rows = [4 * y + other for other in qs]
    z_columns = [4 * other + x for other in zs]
    plane = [(xs[b], (y_rows[a], x_columns[b])) for a in range(8) for b in range(4)][1:]
    group = [(xs[b], qs[a], (q_rows[a], x_columns[b])) for b in range(4) for a in range(4)][1:]
    in_core = [(4 * y + 2 * lax.rem(half_q + a, 2) + core, x_columns[b]) for b in range(4) for a in range(2)][1:]

    def in_y(i):
        return (y_rows[i], n)

    def in_z(i):
        return (w, z_columns[i])

    def in_q(i):
        return (q_rows[i], n)

    barrier = pltpu.get_barrier_semaphore()

    def greet(device):
        pl.semaphore_signal(barrier, inc=1, device_id=device, device_id_type=MESH)

    @pl.when(jnp.logical_not(own_basis))
    def _():
        greet((basis_source, n))

    @pl.when(beam_source != n)
    def _():
        greet((w, beam_source))

    for item in group:
        greet(item[-1])
    for item in plane:
        greet(item[-1])

    for i in range(1, 4):
        greet(in_z(i))

    @pl.when(gives_basis)
    def _():
        for i in range(4):
            load_block(i).wait()
            basis_t[i] = block_v[i].astype(F32).T.astype(BF16)

    load_fore.wait()
    load_sig.wait()
    column = 4 * w + lax.broadcasted_iota(jnp.int32, (4, 256), 0)
    for f in range(8):
        low = start_ref[f]
        inband = ((column >= low) & (column < low + width_ref[f])).astype(F32)
        spec[own, pl.ds(4 * f, 4), :] = fore_v[f] + inband * sig_v[f]

    expected = 16 * gives_basis.astype(jnp.int32) - own_basis.astype(jnp.int32) + gives_beams.astype(jnp.int32) * (8 - own_beam.astype(jnp.int32))
    pl.semaphore_wait(barrier, 49 + expected)

    @pl.when(gives_basis)
    def _():
        for i in range(4):
            for r in range(4):
                other = 16 * core + 4 * i + r
                source = basis_t.at[i, pl.ds(32 * r, 32), :]

                @pl.when(other == w)
                def _():
                    pltpu.make_async_copy(source, basis_in, recv.at[1]).start()

                @pl.when(other != w)
                def _():
                    put(source, basis_in, send.at[1], recv.at[1], (other, n)).start()

    for device in in_core:
        put(spec.at[own], spec.at[own], send.at[0], recv.at[0], device).start()

    quarter = beam_f.at[pl.ds(pl.multiple_of(64 * q, 64), 64), :]

    @pl.when(gives_beams)
    def _():
        for i in range(8):
            other = 4 * (i // 2) + 2 * lax.rem(n, 2) + i % 2
            source = beams_hbm.at[4 * (i % 2) + i // 2, pl.ds(pl.multiple_of(64 * q, 64), 64), :]

            @pl.when(other == n)
            def _():
                pltpu.make_async_copy(source, quarter, recv.at[2]).start()

            @pl.when(other != n)
            def _():
                put(source, quarter, send.at[12], recv.at[2], (w, other)).start()

    @pl.when(q == x)
    def _():
        source = basis_hbm.at[pl.ds(pl.multiple_of(256 * z, 256), 256), :]
        pltpu.make_async_copy(source, basis_f, recv.at[3]).start()
        for i in range(1, 4):
            put(source, basis_f, send.at[3], recv.at[3], in_q(i)).start()

    load_beam.wait()
    drain(basis_in, recv.at[1])
    product = jnp.dot(basis_in[...], beam_v[...], preferred_element_type=F32)
    for r in range(4):
        made[r] = product[8 * r : 8 * r + 8].astype(BF16)

    me = 8 * x + y

    for to_x, device in plane:
        put(made.at[to_x], pieces.at[me], send.at[4], recv.at[4], device).start()

    pieces[me] = made[x]

    drain(spec.at[pl.ds(0, 7)], recv.at[0])
    ours = spec.at[pl.ds(pl.multiple_of(8 * core, 8), 8)]
    put(ours, ours, send.at[13], recv.at[13], sibling).start()

    drain(quarter, recv.at[2])
    for i in range(1, 4):
        put(quarter, quarter, send.at[5], recv.at[5], in_q(i)).start()

    @pl.when(q == x)
    def _():
        pltpu.make_async_copy(quarter, beam_in, recv.at[7]).start()

    @pl.when(q != x)
    def _():
        put(quarter, beam_in, send.at[7], recv.at[7], (4 * y + x, 4 * z + q)).start()

    drain(spec.at[pl.ds(0, 8)], recv.at[13])
    drain(pieces.at[pl.ds(0, 31)], recv.at[4])

    for i in range(32):
        wide[i] = pieces[i].astype(F32)
    for step in (2, 1, 3, 0):
        to_z = zs[step]
        for r in range(4):
            total = None
            for xx in range(4):
                for f in range(8):
                    item = spec[8 * (r % 2) + 2 * xx + r // 2, pl.ds(4 * f + to_z, 1), :] * wide[8 * xx + f]
                    total = item if total is None else total + item
            part[to_z, r] = total.astype(BF16)
        if step:
            put(part.at[to_z], got.at[z], send.at[6], recv.at[6], (w, 4 * to_z + x)).start()

    drain(basis_f, recv.at[3])
    lanes = pl.ds(pl.multiple_of(32 * q, 32), 32)
    drain(beam_f.at[pl.ds(0, 192), :], recv.at[5])
    flipped[...] = basis_f[...].astype(F32).T
    prod[own] = jnp.dot(flipped[lanes, :].astype(BF16), beam_f[...], preferred_element_type=F32).astype(BF16)

    for device in in_core:
        put(prod.at[own], prod.at[own], send.at[2], recv.at[11], device).start()

    got[z] = part[z]
    drain(prod.at[pl.ds(0, 7)], recv.at[11])
    shared = prod.at[pl.ds(pl.multiple_of(8 * core, 8), 8)]
    put(shared, shared, send.at[14], recv.at[14], sibling).start()
    drain(got.at[pl.ds(0, 3)], recv.at[6])
    drain(prod.at[pl.ds(0, 8)], recv.at[14])

    term = None
    for r in range(4):
        total = (got[0, r].astype(F32) + got[1, r].astype(F32)) + (got[2, r].astype(F32) + got[3, r].astype(F32))
        mine[r] = total
        high, low = split(total)
        for part_of in (high, low):
            item = jnp.concatenate([nt(part_of, prod[8 * (c % 2) + 2 * r + c // 2]) for c in range(4)], axis=1)
            term = item if term is None else term + item
    got6[z] = term

    for i in range(1, 4):
        put(got6.at[z], got6.at[z], send.at[9], recv.at[9], in_z(i)).start()

    place = pl.multiple_of(32 * q + 8 * x, 8)

    for to_x, to_q, device in group:
        put(mine.at[to_q], rows.at[pl.ds(place, 8), :], send.at[8], recv.at[8], device).start()

    rows[pl.ds(place, 8), :] = mine[q]
    drain(got6.at[pl.ds(0, 3)], recv.at[9])
    got7[y] = (got6[0] + got6[1]) + (got6[2] + got6[3])
    for i in range(1, 8):
        put(got7.at[y], got7.at[y], send.at[10], recv.at[10], in_y(i)).start()
    drain(beam_in, recv.at[7])
    drain(rows.at[pl.ds(0, 120)], recv.at[8])
    high, low = split(rows[...])
    chunk = beam_in[...]
    proj_ref[...] = nt(chunk, high) + nt(chunk, low)
    drain(got7.at[pl.ds(0, 7)], recv.at[10])
    total = got7[0]
    for i in range(1, 8):
        total = total + got7[i]
    here = kl_v.at[pl.ds(place, 8), :]
    here[...] = total * (1.0 / 128)

    for item in group:
        put(here, here, send.at[11], recv.at[12], item[-1]).start()

    drain(kl_v.at[pl.ds(0, 120)], recv.at[12])
    kl_ref[...] = kl_v[...]

    drain(spec.at[pl.ds(0, 7)], send.at[0])
    drain(spec.at[pl.ds(0, 8)], send.at[13])

    @pl.when(own_basis)
    def _():
        drain(prod.at[pl.ds(0, 15)], send.at[1])

    @pl.when(gives_basis & jnp.logical_not(own_basis))
    def _():
        drain(prod, send.at[1])

    @pl.when(gives_beams & own_beam)
    def _():
        drain(prod.at[pl.ds(0, 14)], send.at[12])

    @pl.when(gives_beams & jnp.logical_not(own_beam))
    def _():
        drain(prod, send.at[12])

    @pl.when(q == x)
    def _():
        drain(prod.at[pl.ds(0, 12)], send.at[3])

    @pl.when(q != x)
    def _():
        drain(beam_in, send.at[7])

    drain(prod.at[pl.ds(0, 7)], send.at[2])
    drain(prod.at[pl.ds(0, 8)], send.at[14])
    drain(pieces.at[pl.ds(0, 31)], send.at[4])
    drain(beam_f.at[pl.ds(0, 192), :], send.at[5])
    drain(got.at[pl.ds(0, 3)], send.at[6])
    drain(rows.at[pl.ds(0, 120)], send.at[8])
    drain(got6.at[pl.ds(0, 3)], send.at[9])
    drain(got7.at[pl.ds(0, 7)], send.at[10])
    drain(kl_v.at[pl.ds(0, 120)], send.at[11])


def per_device(beams, basis, foreground, signal, band_start, band_width):
    anywhere = pl.BlockSpec(memory_space=pl.ANY)
    scalars = pl.BlockSpec(memory_space=pltpu.SMEM)
    vector = pl.BlockSpec(memory_space=pltpu.VMEM)
    return pl.pallas_call(
        kernel,
        out_shape=(
            pltpu.VMEM((64, 128), F32),
            pltpu.VMEM((128, 128), F32),
        ),
        in_specs=[anywhere] * 4 + [scalars] * 2,
        out_specs=(vector, vector),
        scratch_shapes=[
            pltpu.VMEM((256, 256), BF16),
            pltpu.VMEM((4, 256, 128), BF16),
            pltpu.VMEM((8, 4, 256), F32),
            pltpu.VMEM((8, 4, 256), F32),
            pltpu.VMEM((4, 128, 256), BF16),
            pltpu.VMEM((32, 256), BF16),
            pltpu.VMEM((4, 8, 256), BF16),
            pltpu.VMEM((32, 8, 256), BF16),
            pltpu.VMEM((32, 8, 256), F32),
            pltpu.VMEM((256, 256), BF16),
            pltpu.VMEM((256, 128), BF16),
            pltpu.VMEM((128, 256), F32),
            pltpu.VMEM((64, 256), BF16),
            pltpu.VMEM((16, 32, 256), BF16),
            pltpu.VMEM((16, 32, 256), F32),
            pltpu.VMEM((4, 4, 8, 256), BF16),
            pltpu.VMEM((4, 4, 8, 256), BF16),
            pltpu.VMEM((4, 8, 256), F32),
            pltpu.VMEM((128, 256), F32),
            pltpu.VMEM((4, 8, 128), F32),
            pltpu.VMEM((8, 8, 128), F32),
            pltpu.VMEM((128, 128), F32),
            pltpu.SemaphoreType.DMA((8,)),
            pltpu.SemaphoreType.DMA((15,)),
            pltpu.SemaphoreType.DMA((15,)),
        ],
        compiler_params=pltpu.CompilerParams(
            collective_id=0, has_side_effects=True, vmem_limit_bytes=60 << 20
        ),
    )(beams, basis, foreground, signal, band_start, band_width)


def solution(mesh):
    placed = (
        P("narrow", None, None),
        P("wide", None),
        P("narrow", "wide", None),
        P("narrow", "wide", None),
        P("narrow"),
        P("narrow"),
    )
    return jax.shard_map(
        per_device,
        mesh=mesh,
        in_specs=placed,
        out_specs=(P(("wide", "narrow"), None), P()),
        check_vma=False,
    )
```

```python
import jax
import jax.numpy as jnp
from jax import lax
from jax.experimental import pallas as pl
from jax.experimental.pallas import tpu as pltpu
from jax.sharding import PartitionSpec as P

MESH = pl.DeviceIdType.MESH
F32 = jnp.float32
BF16 = jnp.bfloat16
NT = (((1,), (1,)), ((), ()))


def nt(a, b):
    return lax.dot_general(a, b, NT, preferred_element_type=F32)


def split(value):
    high = value.astype(BF16)
    return high, (value - high.astype(F32)).astype(BF16)


def put(src, dst, send, recv, device):
    return pltpu.make_async_remote_copy(
        src_ref=src, dst_ref=dst, send_sem=send, recv_sem=recv, device_id=device, device_id_type=MESH
    )


def drain(ref, sem):
    pltpu.make_async_copy(ref, ref, sem).wait()


def kernel(
    beams_hbm, basis_hbm, fore_hbm, sig_hbm, start_ref, width_ref, proj_ref, kl_ref,
    beam_v, block_v, fore_v, sig_v, basis_t, basis_in, made, pieces, wide, beam_f, basis_f, flipped, beam_in, prod, spec, part,
    got, mine, rows, got6, got7, kl_v, local, send, recv,
):
    w = lax.axis_index("wide")
    n = lax.axis_index("narrow")
    y, q = lax.div(w, 4), lax.rem(w, 4)
    z, x = lax.div(n, 4), lax.rem(n, 4)
    chip, core = lax.div(w, 2), lax.rem(w, 2)
    g = x * 4 + q
    pair = 2 * x + lax.div(q, 2)
    own = 8 * core + pair
    sibling = (w + 1 - 2 * core, n)

    gives_basis = chip == n
    basis_source = 2 * n + lax.div(y, 4)
    own_basis = basis_source == w
    gives_beams = lax.div(n, 2) == y
    own_beam = (x == 0) | (x == 3)
    beam_source = 2 * y + lax.div(x, 2)

    load_fore = pltpu.make_async_copy(fore_hbm, fore_v, local.at[1])
    load_sig = pltpu.make_async_copy(sig_hbm, sig_v, local.at[2])
    load_beam = pltpu.make_async_copy(beams_hbm.at[y], beam_v, local.at[3])

    def load_block(i):
        return pltpu.make_async_copy(basis_hbm.at[pl.ds(256 * i, 256), :], block_v.at[i], local.at[4 + i])

    @pl.when(gives_basis)
    def _():
        for i in range(4):
            load_block(i).start()

    load_fore.start()
    load_sig.start()
    load_beam.start()

    ys = [lax.rem(y + i, 8) for i in range(8)]
    xs = [lax.rem(x + i, 4) for i in range(4)]
    zs = [lax.rem(z + i, 4) for i in range(4)]
    qs = [lax.rem(q + i, 4) for i in range(4)]
    half_q = lax.div(q, 2)
    y_rows = [4 * other + q for other in ys]
    x_columns = [4 * z + other for other in xs]
    q_rows = [4 * y + other for other in qs]
    z_columns = [4 * other + x for other in zs]
    plane = [(xs[b], (y_rows[a], x_columns[b])) for a in range(8) for b in range(4)][1:]
    group = [(xs[b], qs[a], (q_rows[a], x_columns[b])) for b in range(4) for a in range(4)][1:]
    in_core = [(4 * y + 2 * lax.rem(half_q + a, 2) + core, x_columns[b]) for b in range(4) for a in range(2)][1:]

    def in_y(i):
        return (y_rows[i], n)

    def in_z(i):
        return (w, z_columns[i])

    def in_q(i):
        return (q_rows[i], n)

    barrier = pltpu.get_barrier_semaphore()

    def greet(device):
        pl.semaphore_signal(barrier, inc=1, device_id=device, device_id_type=MESH)

    @pl.when(jnp.logical_not(own_basis))
    def _():
        greet((basis_source, n))

    @pl.when(beam_source != n)
    def _():
        greet((w, beam_source))

    for item in group:
        greet(item[-1])
    for item in plane:
        greet(item[-1])

    for i in range(1, 4):
        greet(in_z(i))

    @pl.when(gives_basis)
    def _():
        for i in range(4):
            load_block(i).wait()
            basis_t[i] = block_v[i].astype(F32).T.astype(BF16)

    load_fore.wait()
    load_sig.wait()
    column = 4 * w + lax.broadcasted_iota(jnp.int32, (4, 256), 0)
    for f in range(8):
        low = start_ref[f]
        inband = ((column >= low) & (column < low + width_ref[f])).astype(F32)
        spec[own, pl.ds(4 * f, 4), :] = fore_v[f] + inband * sig_v[f]

    expected = 16 * gives_basis.astype(jnp.int32) - own_basis.astype(jnp.int32) + gives_beams.astype(jnp.int32) * (8 - own_beam.astype(jnp.int32))
    pl.semaphore_wait(barrier, 49 + expected)

    @pl.when(gives_basis)
    def _():
        for i in range(4):
            for r in range(4):
                other = 16 * core + 4 * i + r
                source = basis_t.at[i, pl.ds(32 * r, 32), :]

                @pl.when(other == w)
                def _():
                    pltpu.make_async_copy(source, basis_in, recv.at[1]).start()

                @pl.when(other != w)
                def _():
                    put(source, basis_in, send.at[1], recv.at[1], (other, n)).start()

    for device in in_core:
        put(spec.at[own], spec.at[own], send.at[0], recv.at[0], device).start()

    quarter = beam_f.at[pl.ds(pl.multiple_of(64 * q, 64), 64), :]

    @pl.when(gives_beams)
    def _():
        for i in range(8):
            other = 4 * (i // 2) + 2 * lax.rem(n, 2) + i % 2
            source = beams_hbm.at[4 * (i % 2) + i // 2, pl.ds(pl.multiple_of(64 * q, 64), 64), :]

            @pl.when(other == n)
            def _():
                pltpu.make_async_copy(source, quarter, recv.at[2]).start()

            @pl.when(other != n)
            def _():
                put(source, quarter, send.at[12], recv.at[2], (w, other)).start()

    @pl.when(q == x)
    def _():
        source = basis_hbm.at[pl.ds(pl.multiple_of(256 * z, 256), 256), :]
        pltpu.make_async_copy(source, basis_f, recv.at[3]).start()
        for i in range(1, 4):
            put(source, basis_f, send.at[3], recv.at[3], in_q(i)).start()

    load_beam.wait()
    drain(basis_in, recv.at[1])
    product = jnp.dot(basis_in[...], beam_v[...], preferred_element_type=F32)
    for r in range(4):
        made[r] = product[8 * r : 8 * r + 8].astype(BF16)

    me = 8 * x + y

    for to_x, device in plane:
        put(made.at[to_x], pieces.at[me], send.at[4], recv.at[4], device).start()

    pieces[me] = made[x]

    drain(spec.at[pl.ds(0, 7)], recv.at[0])
    ours = spec.at[pl.ds(pl.multiple_of(8 * core, 8), 8)]
    put(ours, ours, send.at[13], recv.at[13], sibling).start()

    drain(quarter, recv.at[2])
    for i in range(1, 4):
        put(quarter, quarter, send.at[5], recv.at[5], in_q(i)).start()

    @pl.when(q == x)
    def _():
        pltpu.make_async_copy(quarter, beam_in, recv.at[7]).start()

    @pl.when(q != x)
    def _():
        put(quarter, beam_in, send.at[7], recv.at[7], (4 * y + x, 4 * z + q)).start()

    drain(spec.at[pl.ds(0, 8)], recv.at[13])
    drain(pieces.at[pl.ds(0, 31)], recv.at[4])

    for i in range(32):
        wide[i] = pieces[i].astype(F32)
    for step in (2, 1, 3, 0):
        to_z = zs[step]
        for r in range(4):
            total = None
            for xx in range(4):
                for f in range(8):
                    item = spec[8 * (r % 2) + 2 * xx + r // 2, pl.ds(4 * f + to_z, 1), :] * wide[8 * xx + f]
                    total = item if total is None else total + item
            part[to_z, r] = total.astype(BF16)
        if step:
            put(part.at[to_z], got.at[z], send.at[6], recv.at[6], (w, 4 * to_z + x)).start()

    drain(basis_f, recv.at[3])
    lanes = pl.ds(pl.multiple_of(32 * q, 32), 32)
    drain(beam_f.at[pl.ds(0, 192), :], recv.at[5])
    flipped[...] = basis_f[...].astype(F32).T
    prod[own] = jnp.dot(flipped[lanes, :].astype(BF16), beam_f[...], preferred_element_type=F32).astype(BF16)

    for device in in_core:
        put(prod.at[own], prod.at[own], send.at[2], recv.at[11], device).start()

    got[z] = part[z]
    drain(prod.at[pl.ds(0, 7)], recv.at[11])
    shared = prod.at[pl.ds(pl.multiple_of(8 * core, 8), 8)]
    put(shared, shared, send.at[14], recv.at[14], sibling).start()
    drain(got.at[pl.ds(0, 3)], recv.at[6])
    drain(prod.at[pl.ds(0, 8)], recv.at[14])

    term = None
    for r in range(4):
        total = (got[0, r].astype(F32) + got[1, r].astype(F32)) + (got[2, r].astype(F32) + got[3, r].astype(F32))
        mine[r] = total
        high, low = split(total)
        for part_of in (high, low):
            item = jnp.concatenate([nt(part_of, prod[8 * (c % 2) + 2 * r + c // 2]) for c in range(4)], axis=1)
            term = item if term is None else term + item
    got6[z] = term

    for i in range(1, 4):
        put(got6.at[z], got6.at[z], send.at[9], recv.at[9], in_z(i)).start()

    place = pl.multiple_of(32 * q + 8 * x, 8)

    rows[pl.ds(place, 8), :] = mine[q]
    drain(got6.at[pl.ds(0, 3)], recv.at[9])
    got7[y] = (got6[0] + got6[1]) + (got6[2] + got6[3])
    for i in range(1, 8):
        put(got7.at[y], got7.at[y], send.at[10], recv.at[10], in_y(i)).start()

    for to_x, to_q, device in group:
        put(mine.at[to_q], rows.at[pl.ds(place, 8), :], send.at[8], recv.at[8], device).start()

    drain(beam_in, recv.at[7])
    drain(rows.at[pl.ds(0, 120)], recv.at[8])
    high, low = split(rows[...])
    chunk = beam_in[...]
    proj_ref[...] = nt(chunk, high) + nt(chunk, low)
    drain(got7.at[pl.ds(0, 7)], recv.at[10])
    total = got7[0]
    for i in range(1, 8):
        total = total + got7[i]
    here = kl_v.at[pl.ds(place, 8), :]
    here[...] = total * (1.0 / 128)

    for item in group:
        put(here, here, send.at[11], recv.at[12], item[-1]).start()

    drain(kl_v.at[pl.ds(0, 120)], recv.at[12])
    kl_ref[...] = kl_v[...]

    drain(spec.at[pl.ds(0, 7)], send.at[0])
    drain(spec.at[pl.ds(0, 8)], send.at[13])

    @pl.when(own_basis)
    def _():
        drain(prod.at[pl.ds(0, 15)], send.at[1])

    @pl.when(gives_basis & jnp.logical_not(own_basis))
    def _():
        drain(prod, send.at[1])

    @pl.when(gives_beams & own_beam)
    def _():
        drain(prod.at[pl.ds(0, 14)], send.at[12])

    @pl.when(gives_beams & jnp.logical_not(own_beam))
    def _():
        drain(prod, send.at[12])

    @pl.when(q == x)
    def _():
        drain(prod.at[pl.ds(0, 12)], send.at[3])

    @pl.when(q != x)
    def _():
        drain(beam_in, send.at[7])

    drain(prod.at[pl.ds(0, 7)], send.at[2])
    drain(prod.at[pl.ds(0, 8)], send.at[14])
    drain(pieces.at[pl.ds(0, 31)], send.at[4])
    drain(beam_f.at[pl.ds(0, 192), :], send.at[5])
    drain(got.at[pl.ds(0, 3)], send.at[6])
    drain(rows.at[pl.ds(0, 120)], send.at[8])
    drain(got6.at[pl.ds(0, 3)], send.at[9])
    drain(got7.at[pl.ds(0, 7)], send.at[10])
    drain(kl_v.at[pl.ds(0, 120)], send.at[11])


def per_device(beams, basis, foreground, signal, band_start, band_width):
    anywhere = pl.BlockSpec(memory_space=pl.ANY)
    scalars = pl.BlockSpec(memory_space=pltpu.SMEM)
    vector = pl.BlockSpec(memory_space=pltpu.VMEM)
    return pl.pallas_call(
        kernel,
        out_shape=(
            pltpu.VMEM((64, 128), F32),
            pltpu.VMEM((128, 128), F32),
        ),
        in_specs=[anywhere] * 4 + [scalars] * 2,
        out_specs=(vector, vector),
        scratch_shapes=[
            pltpu.VMEM((256, 256), BF16),
            pltpu.VMEM((4, 256, 128), BF16),
            pltpu.VMEM((8, 4, 256), F32),
            pltpu.VMEM((8, 4, 256), F32),
            pltpu.VMEM((4, 128, 256), BF16),
            pltpu.VMEM((32, 256), BF16),
            pltpu.VMEM((4, 8, 256), BF16),
            pltpu.VMEM((32, 8, 256), BF16),
            pltpu.VMEM((32, 8, 256), F32),
            pltpu.VMEM((256, 256), BF16),
            pltpu.VMEM((256, 128), BF16),
            pltpu.VMEM((128, 256), F32),
            pltpu.VMEM((64, 256), BF16),
            pltpu.VMEM((16, 32, 256), BF16),
            pltpu.VMEM((16, 32, 256), F32),
            pltpu.VMEM((4, 4, 8, 256), BF16),
            pltpu.VMEM((4, 4, 8, 256), BF16),
            pltpu.VMEM((4, 8, 256), F32),
            pltpu.VMEM((128, 256), F32),
            pltpu.VMEM((4, 8, 128), F32),
            pltpu.VMEM((8, 8, 128), F32),
            pltpu.VMEM((128, 128), F32),
            pltpu.SemaphoreType.DMA((8,)),
            pltpu.SemaphoreType.DMA((15,)),
            pltpu.SemaphoreType.DMA((15,)),
        ],
        compiler_params=pltpu.CompilerParams(
            collective_id=0, has_side_effects=True, vmem_limit_bytes=60 << 20
        ),
    )(beams, basis, foreground, signal, band_start, band_width)


def solution(mesh):
    placed = (
        P("narrow", None, None),
        P("wide", None),
        P("narrow", "wide", None),
        P("narrow", "wide", None),
        P("narrow"),
        P("narrow"),
    )
    return jax.shard_map(
        per_device,
        mesh=mesh,
        in_specs=placed,
        out_specs=(P(("wide", "narrow"), None), P()),
        check_vma=False,
    )
```
